512 devices in a mesh: quarter: 4 (over x), row: 8 (over z_lo), col: 16 (over y, z_hi, core).
Axes of the slice: x: 4, y: 4, z: 16 (z_hi: 2, z_lo: 8; z = z_hi * 8 + z_lo), core: 2. Of those that a mesh axis runs over, the one named last changes fastest.
Arguments:
- grad: bfloat16 [4, 4096, 4096], P('quarter', 'row', 'col'), may hold values from -6 to 6
- left_root: bfloat16 [4096, 4096], P('row', 'col'), may hold values from -1 to 3, as said below
- right_root: bfloat16 [4, 4096, 4096], P('quarter', 'row', 'col'), may hold values from -1 to 3, as said below
- momentum: float32 [4, 4096, 4096], P('quarter', 'row', 'col'), may hold values from -6 to 6
- weights: bfloat16 [4, 4096, 4096], P('quarter', 'row', 'col'), may hold values from -6 to 6
Outputs:
- momentum_new: float32 [4, 4096, 4096], P('quarter', 'row', 'col')
- new_weights: bfloat16 [4, 4096, 4096], P(None, ('row', 'quarter'), 'col')
The draws below stay inside these ranges and needn't reach their ends.
Inputs may be any that keep to these rules, and one draw needn't show every extreme that they name: `left_root`: symmetric. `right_root`: each block symmetric.
All inputs are finite; a program needn't handle non-finite values.
Results may differ from the reference program's by a relative error of at most 0.001.
Values may be sent and summed in bfloat16 or wider, within the bound.
No kernel may reach another device: no remote copies, remote signals or barrier semaphores. Data moves between devices by JAX's collectives and lax.ppermute only.
A program may use at most 64 MiB of HBM per device.

```python
import math
import jax
import jax.numpy as jnp

ROWS = 4096
COLS = 4096
QUARTERS = 4


def root_factor(key, order):
    first, second = jax.random.split(key)
    noise = jax.random.normal(first, (order, order), jnp.float32)
    symmetric = (noise + noise.T) * (0.35 / math.sqrt(order))
    diagonal = jnp.exp(jax.random.uniform(second, (order,), jnp.float32, math.log(0.5), math.log(2.0)))
    return symmetric + jnp.diag(diagonal)


def draw_left_root(key, part):
    return root_factor(jax.random.fold_in(key, 11), ROWS).astype(jnp.bfloat16)


def draw_right_root(key, part):
    keys = jax.random.split(jax.random.fold_in(key, 23), QUARTERS)
    blocks = [root_factor(keys[number], COLS) for number in range(QUARTERS)]
    return jnp.stack(blocks).astype(jnp.bfloat16)


def block_levels(own_key, extent, shards, least, largest):
    loudness, own = 1.0, jax.random.fold_in(own_key, 6)
    for axis_at, blocks in shards:
        steps = jnp.exp(jax.random.uniform(jax.random.fold_in(own, axis_at), (blocks,), jnp.float32, least / len(shards), largest / len(shards)))
        loudness = loudness * jnp.repeat(steps, extent[axis_at] // blocks).reshape([-1 if axis == axis_at else 1 for axis in range(len(extent))])
    return loudness


def centred(rng, dims, deviation, most, shards=(), held_as=jnp.bfloat16):
    factor_of = block_levels(rng, dims, shards, -0.22, 0.18) if shards else 1.0
    entries = jax.random.normal(rng, dims, jnp.float32) * deviation * factor_of
    return jnp.minimum(jnp.maximum(entries, -most), most).astype(held_as)


def setup_inputs(seed: int = 0) -> dict:
    splits = jax.random.split(jax.random.key(seed), 6)
    return {
        "grad": centred(splits[0], (QUARTERS, ROWS, COLS), 1.0, 6.0, ((0, 4), (1, 8), (2, 16))),
        "left_root": draw_left_root(jax.random.fold_in(splits[5], 71), 0),
        "right_root": draw_right_root(jax.random.fold_in(splits[5], 71), 0),
        "momentum": centred(splits[3], (QUARTERS, ROWS, COLS), 1.0, 6.0, ((0, 4), (1, 8), (2, 16)), jnp.float32),
        "weights": centred(splits[4], (QUARTERS, ROWS, COLS), 1.0, 6.0, ((0, 4), (1, 8), (2, 16))),
    }


decay_rate = 0.9
step_rate = 0.1


def reference(grad, left_root, right_root, momentum, weights):
    moments = []
    updates = []
    for quarter in range(QUARTERS):
        mixed = jnp.dot(grad[quarter], right_root[quarter], preferred_element_type=jnp.float32).astype(jnp.bfloat16)
        product = jnp.dot(left_root, mixed, preferred_element_type=jnp.float32)
        renewed = decay_rate * momentum[quarter] + (1.0 - decay_rate) * product
        updated = (weights[quarter].astype(jnp.float32) - step_rate * renewed).astype(jnp.bfloat16)
        moments.append(renewed)
        updates.append(updated)
    return jnp.stack(moments), jnp.stack(updates)
```

```python
import jax
import jax.numpy as jnp
from jax import lax
from jax.experimental import pallas as pl
from jax.experimental.pallas import tpu as pltpu
from jax.sharding import Mesh, PartitionSpec as P

decay_rate = 0.9
step_rate = 0.1
AXES = ("quarter", "row", "y", "z_hi", "core")
SWAP = [(0, 1), (1, 0)]


def copies_to_all(piece, axis):
    n = lax.axis_size(axis)
    spread = jnp.broadcast_to(piece[None], (n, *piece.shape))
    return lax.all_to_all(spread, axis, 0, 0, tiled=True)


def row_panel(own, other):
    pieces = []
    for piece in (own, other):
        mine = copies_to_all(piece, "y")
        pieces += [mine, lax.ppermute(mine, "core", SWAP)]
    return pieces


def accumulate(place, pieces, b_ref, acc_ref):
    depth = pieces[0].shape[-1]
    half, core = place[0], place[1]

    @pl.when(pl.program_id(0) == 0)
    def _():
        acc_ref[...] = jnp.zeros_like(acc_ref)

    total = acc_ref[...]
    for n, piece in enumerate(pieces):
        at = 2 * (half if n < 2 else 1 - half) + (core if n % 2 == 0 else 1 - core)
        rows = b_ref[pl.ds(pl.multiple_of(at * depth, depth), depth), :]
        total += jnp.dot(piece[0], rows, preferred_element_type=jnp.float32)
    acc_ref[...] = total


def first_kernel(place, a0, a1, a2, a3, b_ref, o_ref, acc_ref):
    accumulate(place, (a0, a1, a2, a3), b_ref, acc_ref)

    @pl.when(pl.program_id(0) == pl.num_programs(0) - 1)
    def _():
        o_ref[...] = acc_ref[...].astype(o_ref.dtype)


def second_kernel(place, a0, a1, a2, a3, b_ref, m_ref, w_ref, mo_ref, wo_ref, acc_ref):
    accumulate(place, (a0, a1, a2, a3), b_ref, acc_ref)

    @pl.when(pl.program_id(0) == pl.num_programs(0) - 1)
    def _():
        renewed = decay_rate * m_ref[...] + (1.0 - decay_rate) * acc_ref[...]
        mo_ref[...] = renewed
        wo_ref[...] = (w_ref[...].astype(jnp.float32) - step_rate * renewed).astype(wo_ref.dtype)


def call(body, name, place, pieces, right, extra, types):
    steps, rows, depth = pieces[0].shape
    columns = right.shape[1]
    whole = pl.BlockSpec((rows, columns), lambda i, place: (0, 0))
    a = pl.BlockSpec((1, rows, depth), lambda i, place: (i, 0, 0))
    b = pl.BlockSpec((4 * depth, columns), lambda i, place: (i, 0))
    moved = 2 * (4 * steps * rows * depth + right.size) + 6 * rows * columns
    return pl.pallas_call(
        body,
        out_shape=[jax.ShapeDtypeStruct((rows, columns), t) for t in types],
        grid_spec=pltpu.PrefetchScalarGridSpec(
            num_scalar_prefetch=1,
            grid=(steps,),
            in_specs=[a] * 4 + [b] + [whole] * len(extra),
            out_specs=[whole] * len(types),
            scratch_shapes=[pltpu.VMEM((rows, columns), jnp.float32)],
        ),
        cost_estimate=pl.CostEstimate(flops=2 * rows * right.size, bytes_accessed=moved, transcendentals=0),
        name=name,
    )(place, *pieces, right, *extra)


def per_device(grad, left_root, right_root, momentum, weights):
    place = jnp.stack((lax.axis_index("z_hi"), lax.axis_index("core"))).astype(jnp.int32)
    quarter = lax.axis_index("quarter")
    quarters = lax.axis_size("quarter")
    rows, depth = left_root.shape
    part = rows // quarters

    right_panel = lax.all_gather(right_root[0], "row", axis=0, tiled=True)
    grad_other = lax.ppermute(grad[0], "z_hi", SWAP)
    left_part = lax.ppermute(lax.dynamic_slice_in_dim(left_root, quarter * part, part, 0), "z_hi", SWAP)
    (mixed,) = call(first_kernel, "mix", place, row_panel(grad[0], grad_other), right_panel, (), (jnp.bfloat16,))

    mixed, left_own, left_part = lax.optimization_barrier((mixed, left_root, left_part))
    mixed_panel = lax.all_gather(mixed, "row", axis=0, tiled=True)
    left_other = copies_to_all(left_part, "quarter").reshape(rows, depth)
    renewed, updated = call(
        second_kernel,
        "update",
        place,
        row_panel(left_own, left_other),
        mixed_panel,
        (momentum[0], weights[0]),
        (jnp.float32, jnp.bfloat16),
    )
    spread = lax.all_to_all(updated.reshape(quarters, part, depth), "quarter", 0, 0, tiled=True)
    return renewed[None], spread


def solution(mesh):
    fine = Mesh(mesh.devices.reshape(4, 8, 4, 2, 2), AXES)
    placed = P("quarter", "row", ("y", "z_hi", "core"))
    return jax.shard_map(
        per_device,
        mesh=fine,
        in_specs=(placed, P("row", ("y", "z_hi", "core")), placed, placed, placed),
        out_specs=(placed, P(None, ("row", "quarter"), ("y", "z_hi", "core"))),
        check_vma=False,
    )
```

```python
import jax
import jax.numpy as jnp
from jax import lax
from jax.experimental import pallas as pl
from jax.experimental.pallas import tpu as pltpu
from jax.sharding import Mesh, PartitionSpec as P

decay_rate = 0.9
step_rate = 0.1
AXES = ("quarter", "row", "y", "z_hi", "core")
SWAP = [(0, 1), (1, 0)]
CUBE = 4


def copies_to_all(piece, axis):
    n = lax.axis_size(axis)
    spread = jnp.broadcast_to(piece[None], (n, *piece.shape))
    return lax.all_to_all(spread, axis, 0, 0, tiled=True)


def turn(piece, by):
    rows = lax.axis_size("row")
    pairs = [(i, i // CUBE * CUBE + (i + by) % CUBE) for i in range(rows)]
    return lax.ppermute(piece, "row", pairs)


def across(piece):
    rows = lax.axis_size("row")
    return lax.ppermute(piece, "row", [(i, i ^ CUBE) for i in range(rows)])


def cube_slots(piece):
    return [piece] + [turn(piece, by) for by in range(1, CUBE)]


def accumulate(place, pieces, slots, panel_ref, sems):
    half, core, turned = place[0], place[1], place[2]
    depth = pieces[0].shape[-1]

    @pl.when(pl.program_id(0) == 0)
    def _():
        loads = [
            pltpu.make_async_copy(slot, panel_ref.at[lax.rem(turned + CUBE - s, CUBE)], sems.at[s])
            for s, slot in enumerate(slots)
        ]
        for load in loads:
            load.start()
        for load in loads:
            load.wait()

    total = None
    for n, piece in enumerate(pieces):
        at = 2 * pl.program_id(0) + (half if n < 2 else 1 - half)
        first = depth * (core if n % 2 == 0 else 1 - core)
        rows = panel_ref[at, pl.ds(pl.multiple_of(first, depth), depth), :]
        part = jnp.dot(piece[0], rows, preferred_element_type=jnp.float32)
        total = part if total is None else total + part
    return total


def split(refs, extra, outs):
    refs = list(refs)
    pieces, slots, refs = refs[:4], refs[4 : 4 + CUBE], refs[4 + CUBE :]
    return pieces, slots, refs[:extra], refs[extra : extra + outs], refs[extra + outs :]


def half_kernel(place, *refs):
    pieces, slots, _, (o_ref,), (panel_ref, sems) = split(refs, 0, 1)
    total = accumulate(place, pieces, slots, panel_ref, sems)

    @pl.when(pl.program_id(0) == 0)
    def _():
        o_ref[...] = total

    @pl.when(pl.program_id(0) == 1)
    def _():
        o_ref[...] += total


def mix_kernel(place, *refs):
    pieces, slots, (p_ref,), (o_ref,), (panel_ref, sems, acc_ref) = split(refs, 1, 1)
    total = accumulate(place, pieces, slots, panel_ref, sems)

    @pl.when(pl.program_id(0) == 0)
    def _():
        acc_ref[...] = p_ref[...] + total

    @pl.when(pl.program_id(0) == 1)
    def _():
        o_ref[...] = (acc_ref[...] + total).astype(o_ref.dtype)


def update_kernel(place, *refs):
    pieces, slots, (p_ref, m_ref, w_ref), (mo_ref, wo_ref), (panel_ref, sems, acc_ref) = split(refs, 3, 2)
    total = accumulate(place, pieces, slots, panel_ref, sems)

    @pl.when(pl.program_id(0) == 0)
    def _():
        acc_ref[...] = p_ref[...] + total

    @pl.when(pl.program_id(0) == 1)
    def _():
        renewed = decay_rate * m_ref[...] + (1.0 - decay_rate) * (acc_ref[...] + total)
        mo_ref[...] = renewed
        wo_ref[...] = (w_ref[...].astype(jnp.float32) - step_rate * renewed).astype(wo_ref.dtype)


def call(body, place, pieces, slots, extra, types):
    _, rows, depth = pieces[0].shape
    own_rows, columns = slots[0].shape
    whole = pl.BlockSpec((rows, columns), lambda i, place: (0, 0))
    a = pl.BlockSpec((1, rows, depth), lambda i, place: (place[3] + i, 0, 0))
    scratch = [pltpu.VMEM((CUBE, own_rows, columns), jnp.bfloat16), pltpu.SemaphoreType.DMA((CUBE,))]
    if extra:
        scratch.append(pltpu.VMEM((rows, columns), jnp.float32))
    moved = 4 * CUBE * rows * depth + 2 * CUBE * own_rows * columns + 8 * rows * columns
    return pl.pallas_call(
        body,
        out_shape=[jax.ShapeDtypeStruct((rows, columns), t) for t in types],
        grid_spec=pltpu.PrefetchScalarGridSpec(
            num_scalar_prefetch=1,
            grid=(2,),
            in_specs=[a] * 4 + [pl.BlockSpec(memory_space=pl.ANY)] * CUBE + [whole] * len(extra),
            out_specs=[whole] * len(types),
            scratch_shapes=scratch,
        ),
        cost_estimate=pl.CostEstimate(
            flops=2 * rows * CUBE * own_rows * columns, bytes_accessed=moved, transcendentals=0
        ),
    )(place, *pieces, *slots, *extra)


def with_partner(mine):
    return [mine, lax.ppermute(mine, "core", SWAP)]


def per_device(grad, left_root, right_root, momentum, weights):
    half, core, row = (lax.axis_index(a).astype(jnp.int32) for a in ("z_hi", "core", "row"))
    upper = row // CUBE
    near = jnp.stack((half, core, row % CUBE, 2 * upper))
    far = jnp.stack((half, core, row % CUBE, 2 - 2 * upper))
    quarter = lax.axis_index("quarter")
    quarters = lax.axis_size("quarter")
    rows, depth = left_root.shape
    part = rows // quarters
    grad, right_root = grad[0], right_root[0]

    left_part = lax.dynamic_slice_in_dim(left_root, quarter * part, part, 0)
    crossed = lax.ppermute(jnp.concatenate((grad, left_part)), "z_hi", SWAP)
    right_far = across(right_root)
    near_slots = cube_slots(right_root)
    grad_mine = copies_to_all(grad, "y")
    grad_theirs = copies_to_all(crossed[:rows], "y")
    panel = with_partner(grad_mine) + with_partner(grad_theirs)
    far_slots = cube_slots(right_far)
    (begun,) = call(half_kernel, near, panel, near_slots, (), (jnp.float32,))
    (mixed,) = call(mix_kernel, far, panel, far_slots, (begun,), (jnp.bfloat16,))
    left_mine = with_partner(copies_to_all(left_root, "y"))

    mixed, left_part = lax.optimization_barrier((mixed, crossed[rows:]))
    mixed_far = across(mixed)
    near_slots = cube_slots(mixed)
    left_other = copies_to_all(left_part, "quarter").reshape(rows, depth)
    left_theirs = copies_to_all(left_other, "y")
    panel = left_mine + with_partner(left_theirs)
    far_slots = cube_slots(mixed_far)
    (begun,) = call(half_kernel, near, panel, near_slots, (), (jnp.float32,))
    renewed, updated = call(
        update_kernel,
        far,
        panel,
        far_slots,
        (begun, momentum[0], weights[0]),
        (jnp.float32, jnp.bfloat16),
    )
    spread = lax.all_to_all(updated.reshape(quarters, part, depth), "quarter", 0, 0, tiled=True)
    return renewed[None], spread


def solution(mesh):
    fine = Mesh(mesh.devices.reshape(4, 8, 4, 2, 2), AXES)
    placed = P("quarter", "row", ("y", "z_hi", "core"))
    return jax.shard_map(
        per_device,
        mesh=fine,
        in_specs=(placed, P("row", ("y", "z_hi", "core")), placed, placed, placed),
        out_specs=(placed, P(None, ("row", "quarter"), ("y", "z_hi", "core"))),
        check_vma=False,
    )
```

```python
import jax
import jax.numpy as jnp
from jax import lax
from jax.experimental import pallas as pl
from jax.experimental.pallas import tpu as pltpu
from jax.sharding import Mesh, PartitionSpec as P

decay_rate = 0.9
step_rate = 0.1
AXES = ("quarter", "row", "y", "z_hi", "core")
SWAP = [(0, 1), (1, 0)]
CUBE = 4


def copies_to_all(piece, axis):
    n = lax.axis_size(axis)
    spread = jnp.broadcast_to(piece[None], (n, *piece.shape))
    return lax.all_to_all(spread, axis, 0, 0, tiled=True)


def turn(piece, by):
    rows = lax.axis_size("row")
    pairs = [(i, i // CUBE * CUBE + (i + by) % CUBE) for i in range(rows)]
    return lax.ppermute(piece, "row", pairs)


def across(piece):
    rows = lax.axis_size("row")
    return lax.ppermute(piece, "row", [(i, i ^ CUBE) for i in range(rows)])


def cube_slots(piece):
    return [piece] + [turn(piece, by) for by in range(1, CUBE)]


def accumulate(place, step, pieces, slots):
    half, core, turned = place[0], place[1], place[2]
    depth = pieces[0].shape[-1]
    odd = (turned + half) % 2
    total = None
    for n, piece in enumerate(pieces):
        first = pl.multiple_of(depth * (core if n % 2 == 0 else 1 - core), depth)
        even, other = (slot[pl.ds(first, depth), :] for slot in slots[2 * step : 2 * step + 2])
        rows = jnp.where(odd == n // 2, even, other)
        part = jnp.dot(piece[0], rows, preferred_element_type=jnp.float32)
        total = part if total is None else total + part
    return total


def split(refs, extra, outs):
    refs = list(refs)
    pieces, slots, refs = refs[:4], refs[4 : 4 + CUBE], refs[4 + CUBE :]
    return pieces, slots, refs[:extra], refs[extra : extra + outs], refs[extra + outs :]


def half_kernel(place, *refs):
    pieces, slots, _, (o_ref,), _ = split(refs, 0, 1)

    @pl.when(pl.program_id(0) == 0)
    def _():
        o_ref[...] = accumulate(place, 0, pieces, slots)

    @pl.when(pl.program_id(0) == 1)
    def _():
        o_ref[...] += accumulate(place, 1, pieces, slots)


def mix_kernel(place, *refs):
    pieces, slots, (p_ref,), (o_ref,), (acc_ref,) = split(refs, 1, 1)

    @pl.when(pl.program_id(0) == 0)
    def _():
        acc_ref[...] = p_ref[...] + accumulate(place, 0, pieces, slots)

    @pl.when(pl.program_id(0) == 1)
    def _():
        o_ref[...] = (acc_ref[...] + accumulate(place, 1, pieces, slots)).astype(o_ref.dtype)


def update_kernel(place, *refs):
    pieces, slots, (p_ref, m_ref, w_ref), (mo_ref, wo_ref), (acc_ref,) = split(refs, 3, 2)

    @pl.when(pl.program_id(0) == 0)
    def _():
        acc_ref[...] = p_ref[...] + accumulate(place, 0, pieces, slots)

    @pl.when(pl.program_id(0) == 1)
    def _():
        product = acc_ref[...] + accumulate(place, 1, pieces, slots)
        renewed = decay_rate * m_ref[...] + (1.0 - decay_rate) * product
        mo_ref[...] = renewed
        wo_ref[...] = (w_ref[...].astype(jnp.float32) - step_rate * renewed).astype(wo_ref.dtype)


def call(body, place, pieces, at_rows, slots, extra, types):
    depth = pieces[0].shape[-1]
    rows, columns = own_rows, _ = slots[0].shape
    whole = pl.BlockSpec((rows, columns), lambda i, place: (0, 0))

    def piece_spec(theirs, block):
        def at(i, place):
            odd = (place[2] + place[0]) % 2
            back = 2 * i + (1 - odd if theirs else odd)
            return place[3] + (place[2] + 2 * CUBE - back) % CUBE // 2, block, 0

        return pl.BlockSpec((1, rows, depth), at)

    slot_spec = pl.BlockSpec((own_rows, columns), lambda i, place: (0, 0))
    moved = 4 * CUBE * rows * depth + 2 * CUBE * own_rows * columns + 8 * rows * columns
    return pl.pallas_call(
        body,
        out_shape=[jax.ShapeDtypeStruct((rows, columns), t) for t in types],
        grid_spec=pltpu.PrefetchScalarGridSpec(
            num_scalar_prefetch=1,
            grid=(2,),
            in_specs=[piece_spec(n >= 2, at_rows[n]) for n in range(4)] + [slot_spec] * CUBE + [whole] * len(extra),
            out_specs=[whole] * len(types),
            scratch_shapes=[pltpu.VMEM((rows, columns), jnp.float32)] if extra else [],
        ),
        cost_estimate=pl.CostEstimate(
            flops=2 * rows * CUBE * own_rows * columns, bytes_accessed=moved, transcendentals=0
        ),
    )(place, *pieces, *slots, *extra)


def with_partner(mine):
    return [mine, lax.ppermute(mine, "core", SWAP)]


def per_device(grad, left_root, right_root, momentum, weights):
    half, core, row = (lax.axis_index(a).astype(jnp.int32) for a in ("z_hi", "core", "row"))
    upper = row // CUBE
    near = jnp.stack((half, core, row % CUBE, 2 * upper))
    far = jnp.stack((half, core, row % CUBE, 2 - 2 * upper))
    quarter = lax.axis_index("quarter")
    quarters = lax.axis_size("quarter")
    rows, depth = left_root.shape
    part = rows // quarters
    grad, right_root = grad[0], right_root[0]

    left_part = lax.dynamic_slice_in_dim(left_root, quarter * part, part, 0)
    crossed = lax.ppermute(jnp.concatenate((grad, left_part)), "z_hi", SWAP)
    right_far = across(right_root)
    near_slots = cube_slots(right_root)
    mine = with_partner(copies_to_all(jnp.concatenate((grad, left_root)), "y"))
    grad_theirs = copies_to_all(crossed[:rows], "y")
    panel = mine + with_partner(grad_theirs)
    far_slots = cube_slots(right_far)
    (begun,) = call(half_kernel, near, panel, (0, 0, 0, 0), near_slots, (), (jnp.float32,))
    (mixed,) = call(mix_kernel, far, panel, (0, 0, 0, 0), far_slots, (begun,), (jnp.bfloat16,))

    mixed, left_part = lax.optimization_barrier((mixed, crossed[rows:]))
    mixed_far = across(mixed)
    near_slots = cube_slots(mixed)
    left_other = copies_to_all(left_part, "quarter").reshape(rows, depth)
    left_theirs = copies_to_all(left_other, "y")
    panel = mine + with_partner(left_theirs)
    far_slots = cube_slots(mixed_far)
    (begun,) = call(half_kernel, near, panel, (1, 1, 0, 0), near_slots, (), (jnp.float32,))
    renewed, updated = call(
        update_kernel,
        far,
        panel,
        (1, 1, 0, 0),
        far_slots,
        (begun, momentum[0], weights[0]),
        (jnp.float32, jnp.bfloat16),
    )
    spread = lax.all_to_all(updated.reshape(quarters, part, depth), "quarter", 0, 0, tiled=True)
    return renewed[None], spread


def solution(mesh):
    fine = Mesh(mesh.devices.reshape(4, 8, 4, 2, 2), AXES)
    placed = P("quarter", "row", ("y", "z_hi", "core"))
    return jax.shard_map(
        per_device,
        mesh=fine,
        in_specs=(placed, P("row", ("y", "z_hi", "core")), placed, placed, placed),
        out_specs=(placed, P(None, ("row", "quarter"), ("y", "z_hi", "core"))),
        check_vma=False,
    )
```

```python
import jax
import jax.numpy as jnp
from jax import lax
from jax.experimental import pallas as pl
from jax.experimental.pallas import tpu as pltpu
from jax.sharding import Mesh, PartitionSpec as P

decay_rate = 0.9
step_rate = 0.1
AXES = ("quarter", "row", "y", "z_hi", "core")
SWAP = [(0, 1), (1, 0)]
CUBE = 4


def copies_to_all(piece, axis):
    n = lax.axis_size(axis)
    spread = jnp.broadcast_to(piece[None], (n, *piece.shape))
    return lax.all_to_all(spread, axis, 0, 0, tiled=True)


def turn(piece, by):
    rows = lax.axis_size("row")
    pairs = [(i, i // CUBE * CUBE + (i + by) % CUBE) for i in range(rows)]
    return lax.ppermute(piece, "row", pairs)


def across(piece):
    rows = lax.axis_size("row")
    return lax.ppermute(piece, "row", [(i, i ^ CUBE) for i in range(rows)])


def cube_slots(piece):
    return [piece] + [turn(piece, by) for by in range(1, CUBE)]


def accumulate(place, step, pieces, slots):
    half, core, turned = place[0], place[1], place[2]
    depth = pieces[0].shape[-1]
    odd = (turned + half) % 2
    total = None
    for n, piece in enumerate(pieces):
        first = pl.multiple_of(depth * (core if n % 2 == 0 else 1 - core), depth)
        even, other = (slot[pl.ds(first, depth), :] for slot in slots[2 * step : 2 * step + 2])
        rows = jnp.where(odd == n // 2, even, other)
        part = jnp.dot(piece[0], rows, preferred_element_type=jnp.float32)
        total = part if total is None else total + part
    return total


def split(refs, extra, outs):
    refs = list(refs)
    pieces, slots, refs = refs[:4], refs[4 : 4 + CUBE], refs[4 + CUBE :]
    return pieces, slots, refs[:extra], refs[extra : extra + outs], refs[extra + outs :]


def half_kernel(place, *refs):
    pieces, slots, _, (o_ref,), _ = split(refs, 0, 1)

    @pl.when(pl.program_id(0) == 0)
    def _():
        o_ref[...] = accumulate(place, 0, pieces, slots)

    @pl.when(pl.program_id(0) == 1)
    def _():
        o_ref[...] += accumulate(place, 1, pieces, slots)


def update_kernel(place, *refs):
    pieces, slots, (p_ref, m_ref, w_ref), (mo_ref, wo_ref), (acc_ref,) = split(refs, 3, 2)

    @pl.when(pl.program_id(0) == 0)
    def _():
        acc_ref[...] = p_ref[...] + accumulate(place, 0, pieces, slots)

    @pl.when(pl.program_id(0) == 1)
    def _():
        product = acc_ref[...] + accumulate(place, 1, pieces, slots)
        renewed = decay_rate * m_ref[...] + (1.0 - decay_rate) * product
        mo_ref[...] = renewed
        wo_ref[...] = (w_ref[...].astype(jnp.float32) - step_rate * renewed).astype(wo_ref.dtype)


def call(body, place, pieces, at_rows, slots, extra, types):
    depth = pieces[0].shape[-1]
    rows, columns = own_rows, _ = slots[0].shape
    whole = pl.BlockSpec((rows, columns), lambda i, place: (0, 0))

    def piece_spec(theirs, block):
        def at(i, place):
            odd = (place[2] + place[0]) % 2
            back = 2 * i + (1 - odd if theirs else odd)
            return place[3] + (place[2] + 2 * CUBE - back) % CUBE // 2, block, 0

        return pl.BlockSpec((1, rows, depth), at)

    slot_spec = pl.BlockSpec((own_rows, columns), lambda i, place: (0, 0))
    moved = 4 * CUBE * rows * depth + 2 * CUBE * own_rows * columns + 8 * rows * columns
    return pl.pallas_call(
        body,
        out_shape=[jax.ShapeDtypeStruct((rows, columns), t) for t in types],
        grid_spec=pltpu.PrefetchScalarGridSpec(
            num_scalar_prefetch=1,
            grid=(2,),
            in_specs=[piece_spec(n >= 2, at_rows[n]) for n in range(4)] + [slot_spec] * CUBE + [whole] * len(extra),
            out_specs=[whole] * len(types),
            scratch_shapes=[pltpu.VMEM((rows, columns), jnp.float32)] if extra else [],
        ),
        cost_estimate=pl.CostEstimate(
            flops=2 * rows * CUBE * own_rows * columns, bytes_accessed=moved, transcendentals=0
        ),
    )(place, *pieces, *slots, *extra)


def mix_kernel(place, a0, a1, a2, a3, b_ref, o_ref, acc_ref):
    half, core = place[0], place[1]
    depth = a0.shape[-1]
    total = None
    for n, piece in enumerate((a0, a1, a2, a3)):
        at = 2 * (half if n < 2 else 1 - half) + (core if n % 2 == 0 else 1 - core)
        rows = b_ref[pl.ds(pl.multiple_of(at * depth, depth), depth), :]
        part = jnp.dot(piece[0], rows, preferred_element_type=jnp.float32)
        total = part if total is None else total + part

    @pl.when(pl.program_id(0) == 0)
    def _():
        acc_ref[...] = total

    @pl.when(pl.program_id(0) > 0)
    def _():
        acc_ref[...] += total

    @pl.when(pl.program_id(0) == pl.num_programs(0) - 1)
    def _():
        o_ref[...] = acc_ref[...].astype(o_ref.dtype)


def mix(place, pieces, right):
    steps, rows, depth = pieces[2].shape
    columns = right.shape[1]
    whole = pl.BlockSpec((rows, columns), lambda i, place: (0, 0))
    a = pl.BlockSpec((1, rows, depth), lambda i, place: (i, 0, 0))
    b = pl.BlockSpec((4 * depth, columns), lambda i, place: (i, 0))
    return pl.pallas_call(
        mix_kernel,
        out_shape=jax.ShapeDtypeStruct((rows, columns), jnp.bfloat16),
        grid_spec=pltpu.PrefetchScalarGridSpec(
            num_scalar_prefetch=1,
            grid=(steps,),
            in_specs=[a] * 4 + [b],
            out_specs=whole,
            scratch_shapes=[pltpu.VMEM((rows, columns), jnp.float32)],
        ),
        cost_estimate=pl.CostEstimate(
            flops=2 * rows * right.size,
            bytes_accessed=2 * (4 * steps * rows * depth + right.size),
            transcendentals=0,
        ),
        name="mix",
    )(place, *pieces, right)


def with_partner(mine):
    return [mine, lax.ppermute(mine, "core", SWAP)]


def per_device(grad, left_root, right_root, momentum, weights):
    half, core, row = (lax.axis_index(a).astype(jnp.int32) for a in ("z_hi", "core", "row"))
    upper = row // CUBE
    near = jnp.stack((half, core, row % CUBE, 2 * upper))
    far = jnp.stack((half, core, row % CUBE, 2 - 2 * upper))
    quarter = lax.axis_index("quarter")
    quarters = lax.axis_size("quarter")
    rows, depth = left_root.shape
    part = rows // quarters
    grad, right_root = grad[0], right_root[0]

    right_panel = lax.all_gather(right_root, "row", axis=0, tiled=True)
    left_part = lax.dynamic_slice_in_dim(left_root, quarter * part, part, 0)
    crossed = lax.ppermute(jnp.concatenate((grad, left_part)), "z_hi", SWAP)
    mine = with_partner(copies_to_all(jnp.concatenate((grad, left_root)), "y"))
    grad_theirs = copies_to_all(crossed[:rows], "y")
    panel = mine + with_partner(grad_theirs)
    mixed = mix(near, panel, right_panel)
    _, left_part = lax.optimization_barrier((grad_theirs, crossed[rows:]))
    left_other = copies_to_all(left_part, "quarter").reshape(rows, depth)

    mixed, left_other = lax.optimization_barrier((mixed, left_other))
    mixed_far = across(mixed)
    near_slots = cube_slots(mixed)
    left_theirs = copies_to_all(left_other, "y")
    panel = mine + with_partner(left_theirs)
    far_slots = cube_slots(mixed_far)
    (begun,) = call(half_kernel, near, panel, (1, 1, 0, 0), near_slots, (), (jnp.float32,))
    renewed, updated = call(
        update_kernel,
        far,
        panel,
        (1, 1, 0, 0),
        far_slots,
        (begun, momentum[0], weights[0]),
        (jnp.float32, jnp.bfloat16),
    )
    spread = lax.all_to_all(updated.reshape(quarters, part, depth), "quarter", 0, 0, tiled=True)
    return renewed[None], spread


def solution(mesh):
    fine = Mesh(mesh.devices.reshape(4, 8, 4, 2, 2), AXES)
    placed = P("quarter", "row", ("y", "z_hi", "core"))
    return jax.shard_map(
        per_device,
        mesh=fine,
        in_specs=(placed, P("row", ("y", "z_hi", "core")), placed, placed, placed),
        out_specs=(placed, P(None, ("row", "quarter"), ("y", "z_hi", "core"))),
        check_vma=False,
    )
```

```python
import jax
import jax.numpy as jnp
from jax import lax
from jax.experimental import pallas as pl
from jax.experimental.pallas import tpu as pltpu
from jax.sharding import Mesh, PartitionSpec as P

decay_rate = 0.9
step_rate = 0.1
AXES = ("quarter", "row", "y", "z_hi", "core")
SWAP = [(0, 1), (1, 0)]
CUBE = 4


def copies_to_all(piece, axis):
    n = lax.axis_size(axis)
    spread = jnp.broadcast_to(piece[None], (n, *piece.shape))
    return lax.all_to_all(spread, axis, 0, 0, tiled=True)


def turn(piece, by):
    rows = lax.axis_size("row")
    pairs = [(i, i // CUBE * CUBE + (i + by) % CUBE) for i in range(rows)]
    return lax.ppermute(piece, "row", pairs)


def across(piece):
    rows = lax.axis_size("row")
    return lax.ppermute(piece, "row", [(i, i ^ CUBE) for i in range(rows)])


def far_slots(piece):
    return [piece] + [turn(piece, by) for by in range(1, CUBE)]


def accumulate(place, step, pieces, slots):
    half, core, turned = place[0], place[1], place[2]
    depth = pieces[0].shape[-1]
    odd = (turned + half) % 2
    total = None
    for n, piece in enumerate(pieces):
        first = pl.multiple_of(depth * (core if n % 2 == 0 else 1 - core), depth)
        even, other = (
            jnp.concatenate([part[pl.ds(first, depth), :] for part in slot], axis=1)
            for slot in slots[2 * step : 2 * step + 2]
        )
        rows = jnp.where(odd == n // 2, even, other)
        part = jnp.dot(piece[0], rows, preferred_element_type=jnp.float32)
        total = part if total is None else total + part
    return total


def update_kernel(place, *refs):
    pieces, parts, (p_ref, m_ref, w_ref, mo_ref, wo_ref, acc_ref) = refs[:4], refs[4 : 4 + 2 * CUBE], refs[4 + 2 * CUBE :]
    slots = list(zip(parts[:CUBE], parts[CUBE:], strict=True))

    @pl.when(pl.program_id(0) == 0)
    def _():
        acc_ref[...] = p_ref[...] + accumulate(place, 0, pieces, slots)

    @pl.when(pl.program_id(0) == 1)
    def _():
        product = acc_ref[...] + accumulate(place, 1, pieces, slots)
        renewed = decay_rate * m_ref[...] + (1.0 - decay_rate) * product
        mo_ref[...] = renewed
        wo_ref[...] = (w_ref[...].astype(jnp.float32) - step_rate * renewed).astype(wo_ref.dtype)


def update(place, pieces, at_rows, low, high, begun, momentum, weights):
    depth = pieces[0].shape[-1]
    rows, columns = momentum.shape
    whole = pl.BlockSpec((rows, columns), lambda i, place: (0, 0))

    def piece_spec(theirs, block):
        def at(i, place):
            odd = (place[2] + place[0]) % 2
            back = 2 * i + (1 - odd if theirs else odd)
            return place[3] + (place[2] + 2 * CUBE - back) % CUBE // 2, block, 0

        return pl.BlockSpec((1, rows, depth), at)

    slot_spec = pl.BlockSpec(memory_space=pltpu.MemorySpace.VMEM)
    moved = 4 * CUBE * rows * depth + 2 * CUBE * rows * columns + 14 * rows * columns
    return pl.pallas_call(
        update_kernel,
        out_shape=[jax.ShapeDtypeStruct((rows, columns), t) for t in (jnp.float32, jnp.bfloat16)],
        grid_spec=pltpu.PrefetchScalarGridSpec(
            num_scalar_prefetch=1,
            grid=(2,),
            in_specs=[piece_spec(n >= 2, at_rows[n]) for n in range(4)] + [slot_spec] * (2 * CUBE) + [whole] * 3,
            out_specs=[whole, whole],
            scratch_shapes=[pltpu.VMEM((rows, columns), jnp.float32)],
        ),
        cost_estimate=pl.CostEstimate(
            flops=2 * rows * CUBE * rows * columns, bytes_accessed=moved, transcendentals=0
        ),
        name="update",
    )(place, *pieces, *[pltpu.with_memory_space_constraint(v, pltpu.MemorySpace.VMEM) for v in (*low, *high)], begun, momentum, weights)


def mix_kernel(place, a0, a1, a2, a3, b_ref, o_ref, *refs):
    half, core = place[0], place[1]
    depth = a0.shape[-1]
    parts, acc_ref = refs[:-1], refs[-1]
    total = None
    for n, piece in enumerate((a0, a1, a2, a3)):
        at = 2 * (half if n < 2 else 1 - half) + (core if n % 2 == 0 else 1 - core)
        rows = b_ref[pl.ds(pl.multiple_of(at * depth, depth), depth), :]
        part = jnp.dot(piece[0], rows, preferred_element_type=jnp.float32)
        total = part if total is None else total + part

    @pl.when(pl.program_id(0) == 0)
    def _():
        acc_ref[...] = total

    @pl.when(pl.program_id(0) > 0)
    def _():
        acc_ref[...] += total

    @pl.when(pl.program_id(0) == pl.num_programs(0) - 1)
    def _():
        done = acc_ref[...].astype(o_ref.dtype)
        o_ref[...] = done
        for n, part_ref in enumerate(parts):
            width = part_ref.shape[1]
            part_ref[...] = done[:, n * width : (n + 1) * width]


def mix(place, pieces, at_rows, right, kind, split):
    depth = pieces[0].shape[-1]
    columns = right.shape[1]
    steps, rows = right.shape[0] // (4 * depth), 2 * depth
    whole = pl.BlockSpec((rows, columns), lambda i, place: (0, 0))
    block = pl.BlockSpec((rows, columns // max(split, 1)), lambda i, place: (0, 0))
    b = pl.BlockSpec((4 * depth, columns), lambda i, place: (i, 0))

    def piece_spec(at):
        return pl.BlockSpec((1, rows, depth), lambda i, place: (place[3] + i, at, 0))

    return pl.pallas_call(
        mix_kernel,
        out_shape=[jax.ShapeDtypeStruct((rows, columns), kind)]
        + [jax.ShapeDtypeStruct((rows, columns // split), kind) for _ in range(split)],
        grid_spec=pltpu.PrefetchScalarGridSpec(
            num_scalar_prefetch=1,
            grid=(steps,),
            in_specs=[piece_spec(at) for at in at_rows] + [b],
            out_specs=[whole] + [block] * split,
            scratch_shapes=[pltpu.VMEM((rows, columns), jnp.float32)],
        ),
        cost_estimate=pl.CostEstimate(
            flops=2 * rows * right.size,
            bytes_accessed=2 * (4 * steps * rows * depth + right.size),
            transcendentals=0,
        ),
    )(place, *pieces, right)


def with_partner(mine):
    return [mine, lax.ppermute(mine, "core", SWAP)]


def per_device(grad, left_root, right_root, momentum, weights):
    half, core, row = (lax.axis_index(a).astype(jnp.int32) for a in ("z_hi", "core", "row"))
    upper = row // CUBE
    every = jnp.stack((half, core, row % CUBE, 0 * upper))
    near = jnp.stack((half, core, row % CUBE, 2 * upper))
    far = jnp.stack((half, core, row % CUBE, 2 - 2 * upper))
    quarter = lax.axis_index("quarter")
    quarters = lax.axis_size("quarter")
    rows, depth = left_root.shape
    part = rows // quarters
    grad, right_root = grad[0], right_root[0]

    right_panel = lax.all_gather(right_root, "row", axis=0, tiled=True)
    left_part = lax.dynamic_slice_in_dim(left_root, quarter * part, part, 0)
    crossed = lax.ppermute(jnp.concatenate((grad, left_part)), "z_hi", SWAP)
    mine = with_partner(copies_to_all(jnp.concatenate((grad, left_root)), "y"))
    grad_theirs = copies_to_all(crossed[:rows], "y")
    panel = mine + with_partner(grad_theirs)
    mixed, *parts = mix(every, panel, (0, 0, 0, 0), right_panel, jnp.bfloat16, 2)
    _, left_part = lax.optimization_barrier((grad_theirs, crossed[rows:]))
    left_other = copies_to_all(left_part, "quarter").reshape(rows, depth)

    mixed, parts, left_other = lax.optimization_barrier((mixed, parts, left_other))
    runs = [list(range(i, i + CUBE)) for i in range(0, lax.axis_size("row"), CUBE)]
    near_panel = lax.all_gather(mixed, "row", axis=0, tiled=True, axis_index_groups=runs)
    others = []
    for piece in parts:
        others.append(across(piece))
    left_theirs = copies_to_all(left_other, "y")
    panel = mine + with_partner(left_theirs)
    slots = []
    for piece in others:
        slots.append(far_slots(piece))
    (begun,) = mix(near, panel, (1, 1, 0, 0), near_panel, jnp.float32, 0)
    renewed, updated = update(far, panel, (1, 1, 0, 0), *slots, begun, momentum[0], weights[0])
    spread = lax.all_to_all(updated.reshape(quarters, part, depth), "quarter", 0, 0, tiled=True)
    return renewed[None], spread


def solution(mesh):
    fine = Mesh(mesh.devices.reshape(4, 8, 4, 2, 2), AXES)
    placed = P("quarter", "row", ("y", "z_hi", "core"))
    return jax.shard_map(
        per_device,
        mesh=fine,
        in_specs=(placed, P("row", ("y", "z_hi", "core")), placed, placed, placed),
        out_specs=(placed, P(None, ("row", "quarter"), ("y", "z_hi", "core"))),
        check_vma=False,
    )
```

```python
import functools

import jax
import jax.numpy as jnp
from jax import lax
from jax.experimental import pallas as pl
from jax.experimental.pallas import tpu as pltpu
from jax.sharding import Mesh, PartitionSpec as P

decay_rate = 0.9
step_rate = 0.1
AXES = ("quarter", "row", "y", "z_hi", "core")
SWAP = [(0, 1), (1, 0)]
CUBE = 4
KERNEL_VMEM = 16 * 2**20


def copies_to_all(piece, axis):
    n = lax.axis_size(axis)
    spread = jnp.broadcast_to(piece[None], (n, *piece.shape))
    return lax.all_to_all(spread, axis, 0, 0, tiled=True)


def turn(piece, by):
    rows = lax.axis_size("row")
    pairs = [(i, i // CUBE * CUBE + (i + by) % CUBE) for i in range(rows)]
    return lax.ppermute(piece, "row", pairs)


def across(piece):
    rows = lax.axis_size("row")
    return lax.ppermute(piece, "row", [(i, i ^ CUBE) for i in range(rows)])


def far_slots(piece):
    return [piece] + [turn(piece, by) for by in range(1, CUBE)]


def accumulate(place, step, pieces, at_rows, slots):
    half, core, turned = place[0], place[1], place[2]
    depth = pieces[0].shape[-1]
    odd = (turned + half) % 2
    total = None
    for n, piece in enumerate(pieces):
        first = pl.multiple_of(depth * (core if n % 2 == 0 else 1 - core), depth)
        even, other = (
            jnp.concatenate([part[pl.ds(first, depth), :] for part in slot], axis=1)
            for slot in slots[2 * step : 2 * step + 2]
        )
        rows = jnp.where(odd == n // 2, even, other)
        back = 2 * step + (odd if n < 2 else 1 - odd)
        at = place[3] + (turned + 2 * CUBE - back) % CUBE // 2
        block = piece[at, at_rows[n] * 2 * depth : (at_rows[n] + 1) * 2 * depth, :]
        part = jnp.dot(block, rows, preferred_element_type=jnp.float32)
        total = part if total is None else total + part
    return total


def update_kernel(at_rows, place, *refs):
    pieces, parts, (p_ref, m_ref, w_ref, mo_ref, wo_ref) = refs[:4], refs[4 : 4 + 2 * CUBE], refs[4 + 2 * CUBE :]
    slots = list(zip(parts[:CUBE], parts[CUBE:], strict=True))
    product = p_ref[...]
    for step in range(CUBE // 2):
        product += accumulate(place, step, pieces, at_rows, slots)
    renewed = decay_rate * m_ref[...] + (1.0 - decay_rate) * product
    mo_ref[...] = renewed
    wo_ref[...] = (w_ref[...].astype(jnp.float32) - step_rate * renewed).astype(wo_ref.dtype)


def update(place, pieces, at_rows, low, high, begun, momentum, weights):
    depth = pieces[0].shape[-1]
    rows, columns = momentum.shape
    given = in_vmem([*pieces, *low, *high, begun, momentum, weights])
    moved = 4 * CUBE * rows * depth + 2 * CUBE * rows * columns + 14 * rows * columns
    return pl.pallas_call(
        functools.partial(update_kernel, at_rows),
        out_shape=[jax.ShapeDtypeStruct((rows, columns), t) for t in (jnp.float32, jnp.bfloat16)],
        grid_spec=pltpu.PrefetchScalarGridSpec(
            num_scalar_prefetch=1,
            grid=(1,),
            in_specs=[pl.BlockSpec(memory_space=pltpu.MemorySpace.VMEM)] * len(given),
            out_specs=[pl.BlockSpec((rows, columns), lambda i, place: (0, 0))] * 2,
        ),
        cost_estimate=pl.CostEstimate(
            flops=2 * rows * CUBE * rows * columns, bytes_accessed=moved, transcendentals=0
        ),
        compiler_params=pltpu.CompilerParams(vmem_limit_bytes=KERNEL_VMEM),
        name="update",
    )(place, *given)


def mix_kernel(at_rows, place, a0, a1, a2, a3, b_ref, o_ref, acc_ref):
    half, core = place[0], place[1]
    depth = a0.shape[-1]
    at = place[3] + pl.program_id(0)
    total = None
    for n, piece in enumerate((a0, a1, a2, a3)):
        first = 2 * (half if n < 2 else 1 - half) + (core if n % 2 == 0 else 1 - core)
        rows = b_ref[pl.ds(pl.multiple_of(first * depth, depth), depth), :]
        block = piece[at, at_rows[n] * 2 * depth : (at_rows[n] + 1) * 2 * depth, :]
        part = jnp.dot(block, rows, preferred_element_type=jnp.float32)
        total = part if total is None else total + part

    @pl.when(pl.program_id(0) == 0)
    def _():
        acc_ref[...] = total

    @pl.when(pl.program_id(0) > 0)
    def _():
        acc_ref[...] += total

    @pl.when(pl.program_id(0) == pl.num_programs(0) - 1)
    def _():
        o_ref[...] = acc_ref[...].astype(o_ref.dtype)


def mix(place, pieces, at_rows, right, kind, first=0, columns=None):
    depth = pieces[0].shape[-1]
    columns = columns or right.shape[1]
    steps, rows = right.shape[0] // (4 * depth), 2 * depth
    return pl.pallas_call(
        functools.partial(mix_kernel, at_rows),
        out_shape=jax.ShapeDtypeStruct((rows, columns), kind),
        grid_spec=pltpu.PrefetchScalarGridSpec(
            num_scalar_prefetch=1,
            grid=(steps,),
            in_specs=[pl.BlockSpec(memory_space=pltpu.MemorySpace.VMEM)] * 4
            + [pl.BlockSpec((4 * depth, columns), lambda i, place: (i, first))],
            out_specs=pl.BlockSpec((rows, columns), lambda i, place: (0, 0)),
            scratch_shapes=[pltpu.VMEM((rows, columns), jnp.float32)],
        ),
        cost_estimate=pl.CostEstimate(
            flops=2 * rows * right.shape[0] * columns,
            bytes_accessed=2 * (4 * steps * rows * depth + right.shape[0] * columns),
            transcendentals=0,
        ),
        compiler_params=pltpu.CompilerParams(vmem_limit_bytes=KERNEL_VMEM),
    )(place, *in_vmem(pieces), pltpu.with_memory_space_constraint(right, pltpu.MemorySpace.HBM))


def in_vmem(values):
    return [pltpu.with_memory_space_constraint(value, pltpu.MemorySpace.VMEM) for value in values]


def with_partner(mine):
    return [mine, lax.ppermute(mine, "core", SWAP)]


def per_device(grad, left_root, right_root, momentum, weights):
    half, core, row = (lax.axis_index(a).astype(jnp.int32) for a in ("z_hi", "core", "row"))
    upper = row // CUBE
    every = jnp.stack((half, core, row % CUBE, 0 * upper))
    near = jnp.stack((half, core, row % CUBE, 2 * upper))
    far = jnp.stack((half, core, row % CUBE, 2 - 2 * upper))
    quarter = lax.axis_index("quarter")
    quarters = lax.axis_size("quarter")
    rows, depth = left_root.shape
    part = rows // quarters
    grad, right_root = grad[0], right_root[0]

    right_panel = lax.all_gather(right_root, "row", axis=0, tiled=True)
    left_part = lax.dynamic_slice_in_dim(left_root, quarter * part, part, 0)
    crossed = lax.ppermute(jnp.concatenate((grad, left_part)), "z_hi", SWAP)
    mine = with_partner(copies_to_all(jnp.concatenate((grad, left_root)), "y"))
    grad_theirs = copies_to_all(crossed[:rows], "y")
    panel = mine + with_partner(grad_theirs)
    _, left_part = lax.optimization_barrier((grad_theirs, crossed[rows:]))
    left_other = copies_to_all(left_part, "quarter").reshape(rows, depth)

    half_columns = depth // 2
    parts = []
    for n in range(2):
        parts.append(mix(every, panel, (0, 0, 0, 0), right_panel, jnp.bfloat16, n, half_columns))
    parts[0], left_other = lax.optimization_barrier((parts[0], left_other))
    runs = [list(range(i, i + CUBE)) for i in range(0, lax.axis_size("row"), CUBE)]
    near_panel = lax.all_gather(
        jnp.concatenate(parts, axis=1), "row", axis=0, tiled=True, axis_index_groups=runs
    )
    others = []
    for piece in parts:
        others.append(across(piece))
    left_theirs = copies_to_all(left_other, "y")
    panel = mine + with_partner(left_theirs)
    slots = []
    for piece in others:
        slots.append(far_slots(piece))
    begun = mix(near, panel, (1, 1, 0, 0), near_panel, jnp.float32)
    renewed, updated = update(far, panel, (1, 1, 0, 0), *slots, begun, momentum[0], weights[0])
    spread = lax.all_to_all(updated.reshape(quarters, part, depth), "quarter", 0, 0, tiled=True)
    return renewed[None], spread


def solution(mesh):
    fine = Mesh(mesh.devices.reshape(4, 8, 4, 2, 2), AXES)
    placed = P("quarter", "row", ("y", "z_hi", "core"))
    return jax.shard_map(
        per_device,
        mesh=fine,
        in_specs=(placed, P("row", ("y", "z_hi", "core")), placed, placed, placed),
        out_specs=(placed, P(None, ("row", "quarter"), ("y", "z_hi", "core"))),
        check_vma=False,
    )
```

```python
import functools

import jax
import jax.numpy as jnp
from jax import lax
from jax.experimental import pallas as pl
from jax.experimental.pallas import tpu as pltpu
from jax.sharding import Mesh, PartitionSpec as P

decay_rate = 0.9
step_rate = 0.1
AXES = ("quarter", "row", "y", "z_hi", "core")
SWAP = [(0, 1), (1, 0)]
CUBE = 4
KERNEL_VMEM = 16 * 2**20


def copies_to_all(piece, axis):
    n = lax.axis_size(axis)
    spread = jnp.broadcast_to(piece[None], (n, *piece.shape))
    return lax.all_to_all(spread, axis, 0, 0, tiled=True)


def turn(piece, by):
    rows = lax.axis_size("row")
    pairs = [(i, i // CUBE * CUBE + (i + by) % CUBE) for i in range(rows)]
    return lax.ppermute(piece, "row", pairs)


def across(piece):
    rows = lax.axis_size("row")
    return lax.ppermute(piece, "row", [(i, i ^ CUBE) for i in range(rows)])


def far_slots(piece):
    return [piece] + [turn(piece, by) for by in range(1, CUBE)]


def accumulate(place, step, pieces, at_rows, slots):
    half, core, turned = place[0], place[1], place[2]
    depth = pieces[0].shape[-1]
    odd = (turned + half) % 2
    total = None
    for n, piece in enumerate(pieces):
        first = pl.multiple_of(depth * (core if n % 2 == 0 else 1 - core), depth)
        even, other = (
            jnp.concatenate([part[pl.ds(first, depth), :] for part in slot], axis=1)
            for slot in slots[2 * step : 2 * step + 2]
        )
        rows = jnp.where(odd == n // 2, even, other)
        back = 2 * step + (odd if n < 2 else 1 - odd)
        at = place[3] + (turned + 2 * CUBE - back) % CUBE // 2
        block = piece[at, at_rows[n] * 2 * depth : (at_rows[n] + 1) * 2 * depth, :]
        part = jnp.dot(block, rows, preferred_element_type=jnp.float32)
        total = part if total is None else total + part
    return total


def update_kernel(at_rows, place, *refs):
    pieces, parts, (p_ref, m_ref, w_ref, mo_ref, wo_ref) = refs[:4], refs[4 : 4 + 2 * CUBE], refs[4 + 2 * CUBE :]
    slots = list(zip(parts[:CUBE], parts[CUBE:], strict=True))
    product = p_ref[...]
    for step in range(CUBE // 2):
        product += accumulate(place, step, pieces, at_rows, slots)
    renewed = decay_rate * m_ref[...] + (1.0 - decay_rate) * product
    mo_ref[...] = renewed
    wo_ref[...] = (w_ref[...].astype(jnp.float32) - step_rate * renewed).astype(wo_ref.dtype)


def update(place, pieces, at_rows, low, high, begun, momentum, weights):
    depth = pieces[0].shape[-1]
    rows, columns = momentum.shape
    given = in_vmem([*pieces, *low, *high, begun, momentum, weights])
    moved = 4 * CUBE * rows * depth + 2 * CUBE * rows * columns + 14 * rows * columns
    return pl.pallas_call(
        functools.partial(update_kernel, at_rows),
        out_shape=[jax.ShapeDtypeStruct((rows, columns), t) for t in (jnp.float32, jnp.bfloat16)],
        grid_spec=pltpu.PrefetchScalarGridSpec(
            num_scalar_prefetch=1,
            grid=(1,),
            in_specs=[pl.BlockSpec(memory_space=pltpu.MemorySpace.VMEM)] * len(given),
            out_specs=[pl.BlockSpec((rows, columns), lambda i, place: (0, 0))] * 2,
        ),
        cost_estimate=pl.CostEstimate(
            flops=2 * rows * CUBE * rows * columns, bytes_accessed=moved, transcendentals=0
        ),
        compiler_params=pltpu.CompilerParams(vmem_limit_bytes=KERNEL_VMEM),
        name="update",
    )(place, *given)


def mix_kernel(at_rows, place, a0, a1, a2, a3, b_ref, o_ref, *refs):
    half, core = place[0], place[1]
    depth = a0.shape[-1]
    parts, acc_ref = refs[:-1], refs[-1]
    lefts, rights = [], []
    for n, piece in enumerate((a0, a1, a2, a3)):
        first = 2 * (half if n < 2 else 1 - half) + (core if n % 2 == 0 else 1 - core)
        rights.append(b_ref[pl.ds(pl.multiple_of(first * depth, depth), depth), :])
        at = place[3] + pl.program_id(0) if piece.shape[0] > 1 else 0
        start = at_rows[n] * 2 * depth if piece.shape[1] > 2 * depth else 0
        lefts.append(piece[at, start : start + 2 * depth, :])
    total = jnp.dot(
        jnp.concatenate(lefts, axis=1), jnp.concatenate(rights, axis=0), preferred_element_type=jnp.float32
    )

    @pl.when(pl.program_id(0) == 0)
    def _():
        acc_ref[...] = total

    @pl.when(pl.program_id(0) > 0)
    def _():
        acc_ref[...] += total

    @pl.when(pl.program_id(0) == pl.num_programs(0) - 1)
    def _():
        done = acc_ref[...].astype(o_ref.dtype)
        o_ref[...] = done
        for n, part_ref in enumerate(parts):
            width = part_ref.shape[1]
            part_ref[...] = done[:, n * width : (n + 1) * width]


def mix(place, pieces, at_rows, right, kind, split, streamed=()):
    depth = pieces[0].shape[-1]
    columns = right.shape[1]
    steps, rows = right.shape[0] // (4 * depth), 2 * depth

    def piece_spec(n):
        if n in streamed:
            return pl.BlockSpec((1, rows, depth), lambda i, place: (place[3] + i, at_rows[n], 0))
        return pl.BlockSpec(memory_space=pltpu.MemorySpace.VMEM)

    kept = [piece if n in streamed else in_vmem([piece])[0] for n, piece in enumerate(pieces)]
    widths = [columns] + [columns // split] * split if split else [columns]
    return pl.pallas_call(
        functools.partial(mix_kernel, at_rows),
        out_shape=[jax.ShapeDtypeStruct((rows, width), kind) for width in widths],
        grid_spec=pltpu.PrefetchScalarGridSpec(
            num_scalar_prefetch=1,
            grid=(steps,),
            in_specs=[piece_spec(n) for n in range(4)] + [pl.BlockSpec((4 * depth, columns), lambda i, place: (i, 0))],
            out_specs=[pl.BlockSpec((rows, width), lambda i, place: (0, 0)) for width in widths],
            scratch_shapes=[pltpu.VMEM((rows, columns), jnp.float32)],
        ),
        cost_estimate=pl.CostEstimate(
            flops=2 * rows * right.size,
            bytes_accessed=2 * (4 * steps * rows * depth + right.size),
            transcendentals=0,
        ),
        compiler_params=pltpu.CompilerParams(vmem_limit_bytes=KERNEL_VMEM),
    )(place, *kept, pltpu.with_memory_space_constraint(right, pltpu.MemorySpace.HBM))


def in_vmem(values):
    return [pltpu.with_memory_space_constraint(value, pltpu.MemorySpace.VMEM) for value in values]


def with_partner(mine):
    return [mine, lax.ppermute(mine, "core", SWAP)]


def per_device(grad, left_root, right_root, momentum, weights):
    half, core, row = (lax.axis_index(a).astype(jnp.int32) for a in ("z_hi", "core", "row"))
    upper = row // CUBE
    every = jnp.stack((half, core, row % CUBE, 0 * upper))
    near = jnp.stack((half, core, row % CUBE, 2 * upper))
    far = jnp.stack((half, core, row % CUBE, 2 - 2 * upper))
    quarter = lax.axis_index("quarter")
    quarters = lax.axis_size("quarter")
    rows, depth = left_root.shape
    part = rows // quarters
    grad, right_root = grad[0], right_root[0]

    right_panel = lax.all_gather(right_root, "row", axis=0, tiled=True)
    left_part = lax.dynamic_slice_in_dim(left_root, quarter * part, part, 0)
    cut = (rows + part) // 2
    top = lax.ppermute(grad[:cut], "z_hi", SWAP)
    bottom = lax.ppermute(jnp.concatenate((grad[cut:], left_part)), "z_hi", SWAP)
    mine = with_partner(copies_to_all(jnp.concatenate((grad, left_root)), "y"))
    grad_theirs = copies_to_all(jnp.concatenate((top, bottom[: rows - cut])), "y")
    panel = mine + with_partner(grad_theirs)
    _, left_part = lax.optimization_barrier((grad_theirs, bottom[rows - cut :]))
    left_other = copies_to_all(left_part, "quarter").reshape(rows, depth)

    mixed, *parts = mix(every, panel, (0, 0, 0, 0), right_panel, jnp.bfloat16, 2)
    mixed, parts, left_other = lax.optimization_barrier((mixed, parts, left_other))
    runs = [list(range(i, i + CUBE)) for i in range(0, lax.axis_size("row"), CUBE)]
    near_panel = lax.all_gather(mixed, "row", axis=0, tiled=True, axis_index_groups=runs)
    others = []
    for piece in parts:
        others.append(across(piece))
    left_theirs = copies_to_all(left_other, "y")
    panel = mine + with_partner(left_theirs)
    slots = []
    for piece in others:
        slots.append(far_slots(piece))
    (begun,) = mix(near, panel, (1, 1, 0, 0), near_panel, jnp.float32, 0, (3,))
    renewed, updated = update(far, panel, (1, 1, 0, 0), *slots, begun, momentum[0], weights[0])
    spread = lax.all_to_all(updated.reshape(quarters, part, depth), "quarter", 0, 0, tiled=True)
    return renewed[None], spread


def solution(mesh):
    fine = Mesh(mesh.devices.reshape(4, 8, 4, 2, 2), AXES)
    placed = P("quarter", "row", ("y", "z_hi", "core"))
    return jax.shard_map(
        per_device,
        mesh=fine,
        in_specs=(placed, P("row", ("y", "z_hi", "core")), placed, placed, placed),
        out_specs=(placed, P(None, ("row", "quarter"), ("y", "z_hi", "core"))),
        check_vma=False,
    )
```

```python
import functools

import jax
import jax.numpy as jnp
from jax import lax
from jax.experimental import pallas as pl
from jax.experimental.pallas import tpu as pltpu
from jax.sharding import Mesh, PartitionSpec as P

decay_rate = 0.9
step_rate = 0.1
AXES = ("quarter", "row", "y", "z_hi", "core")
SWAP = [(0, 1), (1, 0)]
CUBE = 4
KERNEL_VMEM = 16 * 2**20


def copies_to_all(piece, axis):
    n = lax.axis_size(axis)
    spread = jnp.broadcast_to(piece[None], (n, *piece.shape))
    return lax.all_to_all(spread, axis, 0, 0, tiled=True)


def y_slots(piece):
    n = lax.axis_size("y")
    return jnp.stack(
        [piece] + [lax.ppermute(piece, "y", [(i, (i + by) % n) for i in range(n)]) for by in range(1, n)]
    )


def turn(piece, by):
    rows = lax.axis_size("row")
    pairs = [(i, i // CUBE * CUBE + (i + by) % CUBE) for i in range(rows)]
    return lax.ppermute(piece, "row", pairs)


def across(piece):
    rows = lax.axis_size("row")
    return lax.ppermute(piece, "row", [(i, i ^ CUBE) for i in range(rows)])


def cube_slots(piece):
    return [piece] + [turn(piece, by) for by in range(1, CUBE)]


def line_slots(piece):
    rows = lax.axis_size("row")
    up, down = [piece], [piece]
    for _ in range(1, rows):
        up.append(lax.ppermute(up[-1], "row", [(i, i + 1) for i in range(rows - 1)]))
        down.append(lax.ppermute(down[-1], "row", [(i + 1, i) for i in range(rows - 1)]))
    return up + down[1:]


def accumulate(place, step, pieces, at_rows, slots):
    half, core, turned = place[0], place[1], place[2]
    depth = pieces[0].shape[-1]
    odd = (turned + half) % 2
    total = None
    for n, piece in enumerate(pieces):
        first = pl.multiple_of(depth * (core if n % 2 == 0 else 1 - core), depth)
        even, other = (
            jnp.concatenate([part[pl.ds(first, depth), :] for part in slot], axis=1)
            for slot in slots[2 * step : 2 * step + 2]
        )
        rows = jnp.where(odd == n // 2, even, other)
        back = 2 * step + (odd if n < 2 else 1 - odd)
        at = place[3] + (turned + 2 * CUBE - back) % CUBE // 2
        if n < 2:
            at = (place[4] + CUBE - at) % CUBE
        block = piece[at, at_rows[n] * 2 * depth : (at_rows[n] + 1) * 2 * depth, :]
        part = jnp.dot(block, rows, preferred_element_type=jnp.float32)
        total = part if total is None else total + part
    return total


def update_kernel(at_rows, place, *refs):
    pieces, parts, (p_ref, m_ref, w_ref, mo_ref, wo_ref) = refs[:4], refs[4 : 4 + 2 * CUBE], refs[4 + 2 * CUBE :]
    slots = list(zip(parts[:CUBE], parts[CUBE:], strict=True))
    product = p_ref[...]
    for step in range(CUBE // 2):
        product += accumulate(place, step, pieces, at_rows, slots)
    renewed = decay_rate * m_ref[...] + (1.0 - decay_rate) * product
    mo_ref[...] = renewed
    wo_ref[...] = (w_ref[...].astype(jnp.float32) - step_rate * renewed).astype(wo_ref.dtype)


def update(place, pieces, at_rows, low, high, begun, momentum, weights):
    depth = pieces[0].shape[-1]
    rows, columns = momentum.shape
    given = in_vmem([*pieces, *low, *high, begun, momentum, weights])
    moved = 4 * CUBE * rows * depth + 2 * CUBE * rows * columns + 14 * rows * columns
    return pl.pallas_call(
        functools.partial(update_kernel, at_rows),
        out_shape=[jax.ShapeDtypeStruct((rows, columns), t) for t in (jnp.float32, jnp.bfloat16)],
        grid_spec=pltpu.PrefetchScalarGridSpec(
            num_scalar_prefetch=1,
            grid=(1,),
            in_specs=[pl.BlockSpec(memory_space=pltpu.MemorySpace.VMEM)] * len(given),
            out_specs=[pl.BlockSpec((rows, columns), lambda i, place: (0, 0))] * 2,
        ),
        cost_estimate=pl.CostEstimate(
            flops=2 * rows * CUBE * rows * columns, bytes_accessed=moved, transcendentals=0
        ),
        compiler_params=pltpu.CompilerParams(vmem_limit_bytes=KERNEL_VMEM),
        name="update",
    )(place, *given)


def mix_kernel(n_rows, place, *refs):
    pieces, slots, outs, panel_ref, sems = refs[:4], refs[4 : 3 + 2 * n_rows], refs[3 + 2 * n_rows : -2], refs[-2], refs[-1]
    half, core, row, y = place[0], place[1], place[2], place[3]
    depth = pieces[0].shape[-1]
    rows = 2 * depth
    for back in range(n_rows):

        @pl.when(row >= back)
        def _():
            pltpu.make_async_copy(slots[back], panel_ref.at[back], sems.at[back]).start()

        if back:

            @pl.when(row < back)
            def _():
                source = slots[2 * n_rows - 1 - back]
                pltpu.make_async_copy(source, panel_ref.at[back], sems.at[back]).start()

    total = None
    for back in range(n_rows):
        pltpu.make_async_copy(slots[back], panel_ref.at[back], sems.at[back]).wait()
        at = (row + n_rows - back) % n_rows
        theirs = (at + half) % 2 == 1
        turned = (y + CUBE - at // 2) % CUBE
        lefts, rights = [], []
        for n in range(2):
            first = pl.multiple_of(depth * (core if n == 0 else 1 - core), depth)
            lefts.append(jnp.where(theirs, pieces[2 + n][turned, :rows, :], pieces[n][turned, :rows, :]))
            rights.append(panel_ref[back, pl.ds(first, depth), :])
        part = jnp.dot(
            jnp.concatenate(lefts, axis=1), jnp.concatenate(rights, axis=0), preferred_element_type=jnp.float32
        )
        total = part if total is None else total + part
    done = total.astype(outs[0].dtype)
    outs[0][...] = done
    for n, part_ref in enumerate(outs[1:]):
        width = part_ref.shape[1]
        part_ref[...] = done[:, n * width : (n + 1) * width]


def mix(place, pieces, slots):
    n_rows = (len(slots) + 1) // 2
    rows, columns = slots[0].shape
    widths = (columns, columns // 2, columns // 2)
    kept = [pltpu.with_memory_space_constraint(slot, pltpu.MemorySpace.HBM) for slot in slots]
    return pl.pallas_call(
        functools.partial(mix_kernel, n_rows),
        out_shape=[jax.ShapeDtypeStruct((rows, width), jnp.bfloat16) for width in widths],
        grid_spec=pltpu.PrefetchScalarGridSpec(
            num_scalar_prefetch=1,
            grid=(1,),
            in_specs=[pl.BlockSpec(memory_space=pltpu.MemorySpace.VMEM)] * 4
            + [pl.BlockSpec(memory_space=pl.ANY)] * len(slots),
            out_specs=[pl.BlockSpec((rows, width), lambda i, place: (0, 0)) for width in widths],
            scratch_shapes=[pltpu.VMEM((n_rows, rows, columns), jnp.bfloat16), pltpu.SemaphoreType.DMA((n_rows,))],
        ),
        cost_estimate=pl.CostEstimate(
            flops=2 * n_rows * rows * rows * columns, bytes_accessed=2 * n_rows * rows * columns, transcendentals=0
        ),
        compiler_params=pltpu.CompilerParams(vmem_limit_bytes=KERNEL_VMEM),
        name="mix",
    )(place, *in_vmem(pieces), *kept)


def near_kernel(at_rows, place, *refs):
    pieces, slots, o_ref = refs[:4], [(slot,) for slot in refs[4:-1]], refs[-1]
    total = None
    for step in range(CUBE // 2):
        part = accumulate(place, step, pieces, at_rows, slots)
        total = part if total is None else total + part
    o_ref[...] = total


def call(body, place, given, widths, kind, flops):
    rows = given[-1].shape[0]
    return pl.pallas_call(
        body,
        out_shape=[jax.ShapeDtypeStruct((rows, width), kind) for width in widths],
        grid_spec=pltpu.PrefetchScalarGridSpec(
            num_scalar_prefetch=1,
            grid=(1,),
            in_specs=[pl.BlockSpec(memory_space=pltpu.MemorySpace.VMEM)] * len(given),
            out_specs=[pl.BlockSpec((rows, width), lambda i, place: (0, 0)) for width in widths],
        ),
        cost_estimate=pl.CostEstimate(flops=flops, bytes_accessed=4 * rows * sum(widths), transcendentals=0),
        compiler_params=pltpu.CompilerParams(vmem_limit_bytes=KERNEL_VMEM),
    )(place, *in_vmem(given))


def in_vmem(values):
    return [pltpu.with_memory_space_constraint(value, pltpu.MemorySpace.VMEM) for value in values]


def with_partner(mine):
    return [mine, lax.ppermute(mine, "core", SWAP)]


def per_device(grad, left_root, right_root, momentum, weights):
    half, core, row = (lax.axis_index(a).astype(jnp.int32) for a in ("z_hi", "core", "row"))
    upper = row // CUBE
    y = lax.axis_index("y").astype(jnp.int32)
    line = jnp.stack((half, core, row, y))
    near = jnp.stack((half, core, row % CUBE, 2 * upper, y))
    far = jnp.stack((half, core, row % CUBE, 2 - 2 * upper, y))
    quarter = lax.axis_index("quarter")
    quarters = lax.axis_size("quarter")
    rows, depth = left_root.shape
    part = rows // quarters
    grad, right_root = grad[0], right_root[0]

    right_slots = line_slots(right_root)
    left_part = lax.dynamic_slice_in_dim(left_root, quarter * part, part, 0)
    crossed = lax.ppermute(jnp.concatenate((grad, left_part)), "z_hi", SWAP)
    mine = y_slots(jnp.concatenate((grad, left_root)))
    mine = with_partner(mine)
    grad_theirs = y_slots(crossed[:rows])
    panel = mine + with_partner(grad_theirs)
    _, left_part = lax.optimization_barrier((grad_theirs, crossed[rows:]))
    left_other = copies_to_all(left_part, "quarter").reshape(rows, depth)

    flops = 2 * rows * rows * CUBE * depth
    mixed, *parts = mix(line, panel, right_slots)
    mixed, parts, left_other = lax.optimization_barrier((mixed, parts, left_other))
    others = []
    for piece in parts:
        others.append(across(piece))
    near_slots = cube_slots(mixed)
    left_theirs = copies_to_all(left_other, "y")
    panel = mine + with_partner(left_theirs)
    slots = []
    for piece in others:
        slots.append(cube_slots(piece))
    (begun,) = call(
        functools.partial(near_kernel, (1, 1, 0, 0)), near, panel + near_slots, (depth,), jnp.float32, flops
    )
    renewed, updated = update(far, panel, (1, 1, 0, 0), *slots, begun, momentum[0], weights[0])
    spread = lax.all_to_all(updated.reshape(quarters, part, depth), "quarter", 0, 0, tiled=True)
    return renewed[None], spread


def solution(mesh):
    fine = Mesh(mesh.devices.reshape(4, 8, 4, 2, 2), AXES)
    placed = P("quarter", "row", ("y", "z_hi", "core"))
    return jax.shard_map(
        per_device,
        mesh=fine,
        in_specs=(placed, P("row", ("y", "z_hi", "core")), placed, placed, placed),
        out_specs=(placed, P(None, ("row", "quarter"), ("y", "z_hi", "core"))),
        check_vma=False,
    )
```

```python
import functools

import jax
import jax.numpy as jnp
from jax import lax
from jax.experimental import pallas as pl
from jax.experimental.pallas import tpu as pltpu
from jax.sharding import Mesh, PartitionSpec as P

decay_rate = 0.9
step_rate = 0.1
AXES = ("quarter", "row", "y", "z_hi", "core")
SWAP = [(0, 1), (1, 0)]
CUBE = 4
KERNEL_VMEM = 16 * 2**20


def copies_to_all(piece, axis):
    n = lax.axis_size(axis)
    spread = jnp.broadcast_to(piece[None], (n, *piece.shape))
    return lax.all_to_all(spread, axis, 0, 0, tiled=True)


def y_slots(piece):
    n = lax.axis_size("y")
    return jnp.stack(
        [piece] + [lax.ppermute(piece, "y", [(i, (i + by) % n) for i in range(n)]) for by in range(1, n)]
    )


def turn(piece, by):
    rows = lax.axis_size("row")
    pairs = [(i, i // CUBE * CUBE + (i + by) % CUBE) for i in range(rows)]
    return lax.ppermute(piece, "row", pairs)


def across(piece):
    rows = lax.axis_size("row")
    return lax.ppermute(piece, "row", [(i, i ^ CUBE) for i in range(rows)])


def far_slots(piece):
    return [piece] + [turn(piece, by) for by in range(1, CUBE)]


def accumulate(place, step, pieces, at_rows, slots):
    half, core, turned = place[0], place[1], place[2]
    depth = pieces[0].shape[-1]
    odd = (turned + half) % 2
    total = None
    for n, piece in enumerate(pieces):
        first = pl.multiple_of(depth * (core if n % 2 == 0 else 1 - core), depth)
        even, other = (
            jnp.concatenate([part[pl.ds(first, depth), :] for part in slot], axis=1)
            for slot in slots[2 * step : 2 * step + 2]
        )
        rows = jnp.where(odd == n // 2, even, other)
        back = 2 * step + (odd if n < 2 else 1 - odd)
        at = place[3] + (turned + 2 * CUBE - back) % CUBE // 2
        if n < 2:
            at = (place[4] + CUBE - at) % CUBE
        block = piece[at, at_rows[n] * 2 * depth : (at_rows[n] + 1) * 2 * depth, :]
        part = jnp.dot(block, rows, preferred_element_type=jnp.float32)
        total = part if total is None else total + part
    return total


def update_kernel(at_rows, place, *refs):
    pieces, parts, (p_ref, m_ref, w_ref, mo_ref, wo_ref) = refs[:4], refs[4 : 4 + 2 * CUBE], refs[4 + 2 * CUBE :]
    slots = list(zip(parts[:CUBE], parts[CUBE:], strict=True))
    product = p_ref[...]
    for step in range(CUBE // 2):
        product += accumulate(place, step, pieces, at_rows, slots)
    renewed = decay_rate * m_ref[...] + (1.0 - decay_rate) * product
    mo_ref[...] = renewed
    wo_ref[...] = (w_ref[...].astype(jnp.float32) - step_rate * renewed).astype(wo_ref.dtype)


def update(place, pieces, at_rows, low, high, begun, momentum, weights):
    depth = pieces[0].shape[-1]
    rows, columns = momentum.shape
    given = in_vmem([*pieces, *low, *high, begun, momentum, weights])
    moved = 4 * CUBE * rows * depth + 2 * CUBE * rows * columns + 14 * rows * columns
    return pl.pallas_call(
        functools.partial(update_kernel, at_rows),
        out_shape=[jax.ShapeDtypeStruct((rows, columns), t) for t in (jnp.float32, jnp.bfloat16)],
        grid_spec=pltpu.PrefetchScalarGridSpec(
            num_scalar_prefetch=1,
            grid=(1,),
            in_specs=[pl.BlockSpec(memory_space=pltpu.MemorySpace.VMEM)] * len(given),
            out_specs=[pl.BlockSpec((rows, columns), lambda i, place: (0, 0))] * 2,
        ),
        cost_estimate=pl.CostEstimate(
            flops=2 * rows * CUBE * rows * columns, bytes_accessed=moved, transcendentals=0
        ),
        compiler_params=pltpu.CompilerParams(vmem_limit_bytes=KERNEL_VMEM),
        name="update",
    )(place, *given)


def mix_kernel(at_rows, place, a0, a1, a2, a3, b_ref, o_ref, *refs):
    half, core = place[0], place[1]
    depth = a0.shape[-1]
    parts, acc_ref = refs[:-1], refs[-1]
    lefts, rights = [], []
    for n, piece in enumerate((a0, a1, a2, a3)):
        first = 2 * (half if n < 2 else 1 - half) + (core if n % 2 == 0 else 1 - core)
        rights.append(b_ref[pl.ds(pl.multiple_of(first * depth, depth), depth), :])
        at = place[3] + pl.program_id(0) if piece.shape[0] > 1 else 0
        if n < 2:
            at = (place[4] + CUBE - at) % CUBE
        start = at_rows[n] * 2 * depth if piece.shape[1] > 2 * depth else 0
        lefts.append(piece[at, start : start + 2 * depth, :])
    total = jnp.dot(
        jnp.concatenate(lefts, axis=1), jnp.concatenate(rights, axis=0), preferred_element_type=jnp.float32
    )

    @pl.when(pl.program_id(0) == 0)
    def _():
        acc_ref[...] = total

    @pl.when(pl.program_id(0) > 0)
    def _():
        acc_ref[...] += total

    @pl.when(pl.program_id(0) == pl.num_programs(0) - 1)
    def _():
        done = acc_ref[...].astype(o_ref.dtype)
        o_ref[...] = done
        for n, part_ref in enumerate(parts):
            width = part_ref.shape[1]
            part_ref[...] = done[:, n * width : (n + 1) * width]


def mix(place, pieces, at_rows, right, kind, split, streamed=()):
    depth = pieces[0].shape[-1]
    columns = right.shape[1]
    steps, rows = right.shape[0] // (4 * depth), 2 * depth

    def piece_spec(n):
        if n in streamed:
            return pl.BlockSpec((1, rows, depth), lambda i, place: (place[3] + i, at_rows[n], 0))
        return pl.BlockSpec(memory_space=pltpu.MemorySpace.VMEM)

    kept = [piece if n in streamed else in_vmem([piece])[0] for n, piece in enumerate(pieces)]
    widths = [columns] + [columns // split] * split if split else [columns]
    return pl.pallas_call(
        functools.partial(mix_kernel, at_rows),
        out_shape=[jax.ShapeDtypeStruct((rows, width), kind) for width in widths],
        grid_spec=pltpu.PrefetchScalarGridSpec(
            num_scalar_prefetch=1,
            grid=(steps,),
            in_specs=[piece_spec(n) for n in range(4)] + [pl.BlockSpec((4 * depth, columns), lambda i, place: (i, 0))],
            out_specs=[pl.BlockSpec((rows, width), lambda i, place: (0, 0)) for width in widths],
            scratch_shapes=[pltpu.VMEM((rows, columns), jnp.float32)],
        ),
        cost_estimate=pl.CostEstimate(
            flops=2 * rows * right.size,
            bytes_accessed=2 * (4 * steps * rows * depth + right.size),
            transcendentals=0,
        ),
        compiler_params=pltpu.CompilerParams(vmem_limit_bytes=KERNEL_VMEM),
    )(place, *kept, pltpu.with_memory_space_constraint(right, pltpu.MemorySpace.HBM))


def in_vmem(values):
    return [pltpu.with_memory_space_constraint(value, pltpu.MemorySpace.VMEM) for value in values]


def with_partner(mine):
    return [mine, lax.ppermute(mine, "core", SWAP)]


def per_device(grad, left_root, right_root, momentum, weights):
    half, core, row = (lax.axis_index(a).astype(jnp.int32) for a in ("z_hi", "core", "row"))
    upper = row // CUBE
    y = lax.axis_index("y").astype(jnp.int32)
    every = jnp.stack((half, core, row % CUBE, 0 * upper, y))
    near = jnp.stack((half, core, row % CUBE, 2 * upper, y))
    far = jnp.stack((half, core, row % CUBE, 2 - 2 * upper, y))
    quarter = lax.axis_index("quarter")
    quarters = lax.axis_size("quarter")
    rows, depth = left_root.shape
    part = rows // quarters
    grad, right_root = grad[0], right_root[0]

    right_panel = lax.all_gather(right_root, "row", axis=0, tiled=True)
    left_part = lax.dynamic_slice_in_dim(left_root, quarter * part, part, 0)
    cuts = (0, 3 * rows // 8, 3 * rows // 4, rows)
    crossed = []
    for start, end in zip(cuts[:-1], cuts[1:], strict=True):
        piece = grad[start:end]
        if end == rows:
            piece = jnp.concatenate((piece, left_part))
        crossed.append(lax.ppermute(piece, "z_hi", SWAP))
    crossed = jnp.concatenate(crossed)
    mine = y_slots(jnp.concatenate((grad, left_root)))
    mine = with_partner(mine)
    grad_theirs = copies_to_all(crossed[:rows], "y")
    panel = mine + with_partner(grad_theirs)
    _, left_part = lax.optimization_barrier((grad_theirs, crossed[rows:]))
    left_other = copies_to_all(left_part, "quarter").reshape(rows, depth)

    mixed, *parts = mix(every, panel, (0, 0, 0, 0), right_panel, jnp.bfloat16, 2)
    mixed, parts, left_other = lax.optimization_barrier((mixed, parts, left_other))
    runs = [list(range(i, i + CUBE)) for i in range(0, lax.axis_size("row"), CUBE)]
    near_panel = lax.all_gather(mixed, "row", axis=0, tiled=True, axis_index_groups=runs)
    others = []
    for piece in parts:
        others.append(across(piece))
    left_theirs = copies_to_all(left_other, "y")
    panel = mine + with_partner(left_theirs)
    slots = []
    for piece in others:
        slots.append(far_slots(piece))
    (begun,) = mix(near, panel, (1, 1, 0, 0), near_panel, jnp.float32, 0, (3,))
    renewed, updated = update(far, panel, (1, 1, 0, 0), *slots, begun, momentum[0], weights[0])
    spread = lax.all_to_all(updated.reshape(quarters, part, depth), "quarter", 0, 0, tiled=True)
    return renewed[None], spread


def solution(mesh):
    fine = Mesh(mesh.devices.reshape(4, 8, 4, 2, 2), AXES)
    placed = P("quarter", "row", ("y", "z_hi", "core"))
    return jax.shard_map(
        per_device,
        mesh=fine,
        in_specs=(placed, P("row", ("y", "z_hi", "core")), placed, placed, placed),
        out_specs=(placed, P(None, ("row", "quarter"), ("y", "z_hi", "core"))),
        check_vma=False,
    )
```

```python
import functools

import jax
import jax.numpy as jnp
from jax import lax
from jax.experimental import pallas as pl
from jax.experimental.pallas import tpu as pltpu
from jax.sharding import Mesh, PartitionSpec as P

decay_rate = 0.9
step_rate = 0.1
AXES = ("quarter", "row", "y", "z_hi", "core")
SWAP = [(0, 1), (1, 0)]
CUBE = 4
KERNEL_VMEM = 16 * 2**20


def copies_to_all(piece, axis):
    n = lax.axis_size(axis)
    spread = jnp.broadcast_to(piece[None], (n, *piece.shape))
    return lax.all_to_all(spread, axis, 0, 0, tiled=True)


def turn(piece, by):
    rows = lax.axis_size("row")
    pairs = [(i, i // CUBE * CUBE + (i + by) % CUBE) for i in range(rows)]
    return lax.ppermute(piece, "row", pairs)


def across(piece):
    rows = lax.axis_size("row")
    return lax.ppermute(piece, "row", [(i, i ^ CUBE) for i in range(rows)])


def far_slots(piece):
    return [piece] + [turn(piece, by) for by in range(1, CUBE)]


def accumulate(place, step, pieces, at_rows, slots):
    half, core, turned = place[0], place[1], place[2]
    depth = pieces[0].shape[-1]
    odd = (turned + half) % 2
    total = None
    for n, piece in enumerate(pieces):
        first = pl.multiple_of(depth * (core if n % 2 == 0 else 1 - core), depth)
        even, other = (slot[pl.ds(first, depth), :] for slot in slots[2 * step : 2 * step + 2])
        rows = jnp.where(odd == n // 2, even, other)
        back = 2 * step + (odd if n < 2 else 1 - odd)
        at = place[3] + (turned + 2 * CUBE - back) % CUBE // 2
        block = piece[at, at_rows[n] * 2 * depth : (at_rows[n] + 1) * 2 * depth, :]
        part = jnp.dot(block, rows, preferred_element_type=jnp.float32)
        total = part if total is None else total + part
    return total


def update_kernel(at_rows, place, *refs):
    pieces, slots, (p_ref, m_ref, w_ref, mo_ref, wo_ref) = refs[:4], refs[4 : 4 + CUBE], refs[4 + CUBE :]
    product = p_ref[...]
    for step in range(CUBE // 2):
        product += accumulate(place, step, pieces, at_rows, slots)
    renewed = decay_rate * m_ref[...] + (1.0 - decay_rate) * product
    mo_ref[...] = renewed
    wo_ref[...] = (w_ref[...].astype(jnp.float32) - step_rate * renewed).astype(wo_ref.dtype)


def update(place, pieces, at_rows, slots, begun, momentum, weights):
    depth = pieces[0].shape[-1]
    rows, columns = momentum.shape
    given = in_vmem([*pieces, *slots, begun, momentum, weights])
    moved = 4 * CUBE * rows * depth + 2 * CUBE * rows * columns + 14 * rows * columns
    return pl.pallas_call(
        functools.partial(update_kernel, at_rows),
        out_shape=[jax.ShapeDtypeStruct((rows, columns), t) for t in (jnp.float32, jnp.bfloat16)],
        grid_spec=pltpu.PrefetchScalarGridSpec(
            num_scalar_prefetch=1,
            grid=(1,),
            in_specs=[pl.BlockSpec(memory_space=pltpu.MemorySpace.VMEM)] * len(given),
            out_specs=[pl.BlockSpec((rows, columns), lambda i, place: (0, 0))] * 2,
        ),
        cost_estimate=pl.CostEstimate(
            flops=2 * rows * CUBE * rows * columns, bytes_accessed=moved, transcendentals=0
        ),
        compiler_params=pltpu.CompilerParams(vmem_limit_bytes=KERNEL_VMEM),
        name="update",
    )(place, *given)


def mix_kernel(at_rows, place, a0, a1, a2, a3, b_ref, o_ref, *refs):
    half, core = place[0], place[1]
    depth = a0.shape[-1]
    parts, acc_ref = refs[:-1], refs[-1]
    lefts, rights = [], []
    for n, piece in enumerate((a0, a1, a2, a3)):
        first = 2 * (half if n < 2 else 1 - half) + (core if n % 2 == 0 else 1 - core)
        rights.append(b_ref[pl.ds(pl.multiple_of(first * depth, depth), depth), :])
        at = place[3] + pl.program_id(0) if piece.shape[0] > 1 else 0
        start = at_rows[n] * 2 * depth if piece.shape[1] > 2 * depth else 0
        lefts.append(piece[at, start : start + 2 * depth, :])
    total = jnp.dot(
        jnp.concatenate(lefts, axis=1), jnp.concatenate(rights, axis=0), preferred_element_type=jnp.float32
    )

    @pl.when(pl.program_id(0) == 0)
    def _():
        acc_ref[...] = total

    @pl.when(pl.program_id(0) > 0)
    def _():
        acc_ref[...] += total

    @pl.when(pl.program_id(0) == pl.num_programs(0) - 1)
    def _():
        done = acc_ref[...].astype(o_ref.dtype)
        o_ref[...] = done
        for n, part_ref in enumerate(parts):
            width = part_ref.shape[1]
            part_ref[...] = done[:, n * width : (n + 1) * width]


def mix(place, pieces, at_rows, right, kind, split, streamed=()):
    depth = pieces[0].shape[-1]
    columns = right.shape[1]
    steps, rows = right.shape[0] // (4 * depth), 2 * depth

    def piece_spec(n):
        if n in streamed:
            return pl.BlockSpec((1, rows, depth), lambda i, place: (place[3] + i, at_rows[n], 0))
        return pl.BlockSpec(memory_space=pltpu.MemorySpace.VMEM)

    kept = [piece if n in streamed else in_vmem([piece])[0] for n, piece in enumerate(pieces)]
    widths = [columns] + [columns // split] * split if split else [columns]
    return pl.pallas_call(
        functools.partial(mix_kernel, at_rows),
        out_shape=[jax.ShapeDtypeStruct((rows, width), kind) for width in widths],
        grid_spec=pltpu.PrefetchScalarGridSpec(
            num_scalar_prefetch=1,
            grid=(steps,),
            in_specs=[piece_spec(n) for n in range(4)] + [pl.BlockSpec((4 * depth, columns), lambda i, place: (i, 0))],
            out_specs=[pl.BlockSpec((rows, width), lambda i, place: (0, 0)) for width in widths],
            scratch_shapes=[pltpu.VMEM((rows, columns), jnp.float32)],
        ),
        cost_estimate=pl.CostEstimate(
            flops=2 * rows * right.size,
            bytes_accessed=2 * (4 * steps * rows * depth + right.size),
            transcendentals=0,
        ),
        compiler_params=pltpu.CompilerParams(vmem_limit_bytes=KERNEL_VMEM),
    )(place, *kept, pltpu.with_memory_space_constraint(right, pltpu.MemorySpace.HBM))


def in_vmem(values):
    return [pltpu.with_memory_space_constraint(value, pltpu.MemorySpace.VMEM) for value in values]


def with_partner(mine):
    return [mine, lax.ppermute(mine, "core", SWAP)]


def per_device(grad, left_root, right_root, momentum, weights):
    half, core, row = (lax.axis_index(a).astype(jnp.int32) for a in ("z_hi", "core", "row"))
    upper = row // CUBE
    every = jnp.stack((half, core, row % CUBE, 0 * upper))
    near = jnp.stack((half, core, row % CUBE, 2 * upper))
    far = jnp.stack((half, core, row % CUBE, 2 - 2 * upper))
    quarter = lax.axis_index("quarter")
    quarters = lax.axis_size("quarter")
    rows, depth = left_root.shape
    part = rows // quarters
    grad, right_root = grad[0], right_root[0]

    right_panel = lax.all_gather(right_root, "row", axis=0, tiled=True)
    left_part = lax.dynamic_slice_in_dim(left_root, quarter * part, part, 0)
    crossed = lax.ppermute(jnp.concatenate((grad, left_part)), "z_hi", SWAP)
    mine = with_partner(copies_to_all(jnp.concatenate((grad, left_root)), "y"))
    grad_theirs = copies_to_all(crossed[:rows], "y")
    panel = mine + with_partner(grad_theirs)
    _, left_part = lax.optimization_barrier((grad_theirs, crossed[rows:]))
    left_other = copies_to_all(left_part, "quarter").reshape(rows, depth)

    (mixed,) = mix(every, panel, (0, 0, 0, 0), right_panel, jnp.bfloat16, 0)
    mixed, left_other = lax.optimization_barrier((mixed, left_other))
    runs = [list(range(i, i + CUBE)) for i in range(0, lax.axis_size("row"), CUBE)]
    near_panel = lax.all_gather(mixed, "row", axis=0, tiled=True, axis_index_groups=runs)
    mixed_far = across(mixed)
    left_theirs = copies_to_all(left_other, "y")
    panel = mine + with_partner(left_theirs)
    slots = far_slots(mixed_far)
    (begun,) = mix(near, panel, (1, 1, 0, 0), near_panel, jnp.float32, 0, (3,))
    renewed, updated = update(far, panel, (1, 1, 0, 0), slots, begun, momentum[0], weights[0])
    spread = lax.all_to_all(updated.reshape(quarters, part, depth), "quarter", 0, 0, tiled=True)
    return renewed[None], spread


def solution(mesh):
    fine = Mesh(mesh.devices.reshape(4, 8, 4, 2, 2), AXES)
    placed = P("quarter", "row", ("y", "z_hi", "core"))
    return jax.shard_map(
        per_device,
        mesh=fine,
        in_specs=(placed, P("row", ("y", "z_hi", "core")), placed, placed, placed),
        out_specs=(placed, P(None, ("row", "quarter"), ("y", "z_hi", "core"))),
        check_vma=False,
    )
```

```python
import functools

import jax
import jax.numpy as jnp
from jax import lax
from jax.experimental import pallas as pl
from jax.experimental.pallas import tpu as pltpu
from jax.sharding import Mesh, PartitionSpec as P

decay_rate = 0.9
step_rate = 0.1
AXES = ("quarter", "row", "y", "z_hi", "core")
SWAP = [(0, 1), (1, 0)]
CUBE = 4
KERNEL_VMEM = 16 * 2**20


def copies_to_all(piece, axis):
    n = lax.axis_size(axis)
    spread = jnp.broadcast_to(piece[None], (n, *piece.shape))
    return lax.all_to_all(spread, axis, 0, 0, tiled=True)


def turn(piece, by):
    rows = lax.axis_size("row")
    pairs = [(i, i // CUBE * CUBE + (i + by) % CUBE) for i in range(rows)]
    return lax.ppermute(piece, "row", pairs)


def across(piece):
    rows = lax.axis_size("row")
    return lax.ppermute(piece, "row", [(i, i ^ CUBE) for i in range(rows)])


def far_slots(piece):
    return [piece] + [turn(piece, by) for by in range(1, CUBE)]


def accumulate(place, step, pieces, at_rows, slots):
    half, core, turned = place[0], place[1], place[2]
    depth = pieces[0].shape[-1]
    odd = (turned + half) % 2
    total = None
    for theirs in range(2):
        back = 2 * step + (1 - odd if theirs else odd)
        at = place[3] + (turned + 2 * CUBE - back) % CUBE // 2
        lefts, rights = [], []
        for n in range(2 * theirs, 2 * theirs + 2):
            first = pl.multiple_of(depth * (core if n % 2 == 0 else 1 - core), depth)
            even, other = (
                jnp.concatenate([part[pl.ds(first, depth), :] for part in slot], axis=1)
                for slot in slots[2 * step : 2 * step + 2]
            )
            rights.append(jnp.where(odd == theirs, even, other))
            lefts.append(pieces[n][at, at_rows[n] * 2 * depth : (at_rows[n] + 1) * 2 * depth, :])
        part = jnp.dot(
            jnp.concatenate(lefts, axis=1), jnp.concatenate(rights, axis=0), preferred_element_type=jnp.float32
        )
        total = part if total is None else total + part
    return total


def update_kernel(at_rows, place, *refs):
    pieces, parts, (p_ref, m_ref, w_ref, mo_ref, wo_ref) = refs[:4], refs[4 : 4 + 2 * CUBE], refs[4 + 2 * CUBE :]
    slots = list(zip(parts[:CUBE], parts[CUBE:], strict=True))
    product = p_ref[...]
    for step in range(CUBE // 2):
        product += accumulate(place, step, pieces, at_rows, slots)
    renewed = decay_rate * m_ref[...] + (1.0 - decay_rate) * product
    mo_ref[...] = renewed
    wo_ref[...] = (w_ref[...].astype(jnp.float32) - step_rate * renewed).astype(wo_ref.dtype)


def update(place, pieces, at_rows, low, high, begun, momentum, weights):
    depth = pieces[0].shape[-1]
    rows, columns = momentum.shape
    given = in_vmem([*pieces, *low, *high, begun, momentum, weights])
    moved = 4 * CUBE * rows * depth + 2 * CUBE * rows * columns + 14 * rows * columns
    return pl.pallas_call(
        functools.partial(update_kernel, at_rows),
        out_shape=[jax.ShapeDtypeStruct((rows, columns), t) for t in (jnp.float32, jnp.bfloat16)],
        grid_spec=pltpu.PrefetchScalarGridSpec(
            num_scalar_prefetch=1,
            grid=(1,),
            in_specs=[pl.BlockSpec(memory_space=pltpu.MemorySpace.VMEM)] * len(given),
            out_specs=[pl.BlockSpec((rows, columns), lambda i, place: (0, 0))] * 2,
        ),
        cost_estimate=pl.CostEstimate(
            flops=2 * rows * CUBE * rows * columns, bytes_accessed=moved, transcendentals=0
        ),
        compiler_params=pltpu.CompilerParams(vmem_limit_bytes=KERNEL_VMEM),
        name="update",
    )(place, *given)


def mix_kernel(at_rows, place, a0, a1, a2, a3, b_ref, o_ref, *refs):
    half, core = place[0], place[1]
    depth = a0.shape[-1]
    parts, acc_ref = refs[:-1], refs[-1]
    lefts, rights = [], []
    per_step = b_ref.shape[0] // (4 * depth)
    for group in range(per_step):
        for n, piece in enumerate((a0, a1, a2, a3)):
            first = 4 * group + 2 * (half if n < 2 else 1 - half) + (core if n % 2 == 0 else 1 - core)
            rights.append(b_ref[pl.ds(pl.multiple_of(first * depth, depth), depth), :])
            streamed = piece.shape[0] == 1
            at = 0 if streamed else place[3] + per_step * pl.program_id(0) + group
            start = 0 if streamed else at_rows[n] * 2 * depth
            lefts.append(piece[at, start : start + 2 * depth, :])
    total = jnp.dot(
        jnp.concatenate(lefts, axis=1), jnp.concatenate(rights, axis=0), preferred_element_type=jnp.float32
    )

    @pl.when(pl.program_id(0) == 0)
    def _():
        acc_ref[...] = total

    @pl.when(pl.program_id(0) > 0)
    def _():
        acc_ref[...] += total

    @pl.when(pl.program_id(0) == pl.num_programs(0) - 1)
    def _():
        done = acc_ref[...].astype(o_ref.dtype)
        o_ref[...] = done
        for n, part_ref in enumerate(parts):
            width = part_ref.shape[1]
            part_ref[...] = done[:, n * width : (n + 1) * width]


def mix(place, pieces, at_rows, right, kind, split, streamed=()):
    depth = pieces[0].shape[-1]
    columns = right.shape[1]
    rows = 2 * depth
    steps = right.shape[0] // (4 * depth if streamed else 8 * depth)
    height = right.shape[0] // steps

    def piece_spec(n):
        if n in streamed:
            return pl.BlockSpec((1, rows, depth), lambda i, place: (place[3] + i, at_rows[n], 0))
        return pl.BlockSpec(memory_space=pltpu.MemorySpace.VMEM)

    kept = [piece if n in streamed else in_vmem([piece])[0] for n, piece in enumerate(pieces)]
    widths = [columns] + [columns // split] * split if split else [columns]
    return pl.pallas_call(
        functools.partial(mix_kernel, at_rows),
        out_shape=[jax.ShapeDtypeStruct((rows, width), kind) for width in widths],
        grid_spec=pltpu.PrefetchScalarGridSpec(
            num_scalar_prefetch=1,
            grid=(steps,),
            in_specs=[piece_spec(n) for n in range(4)] + [pl.BlockSpec((height, columns), lambda i, place: (i, 0))],
            out_specs=[pl.BlockSpec((rows, width), lambda i, place: (0, 0)) for width in widths],
            scratch_shapes=[pltpu.VMEM((rows, columns), jnp.float32)],
        ),
        cost_estimate=pl.CostEstimate(
            flops=2 * rows * right.size,
            bytes_accessed=2 * (right.shape[0] * rows + right.size),
            transcendentals=0,
        ),
        compiler_params=pltpu.CompilerParams(vmem_limit_bytes=KERNEL_VMEM),
    )(place, *kept, pltpu.with_memory_space_constraint(right, pltpu.MemorySpace.HBM))


def in_vmem(values):
    return [pltpu.with_memory_space_constraint(value, pltpu.MemorySpace.VMEM) for value in values]


def with_partner(mine):
    return [mine, lax.ppermute(mine, "core", SWAP)]


def per_device(grad, left_root, right_root, momentum, weights):
    half, core, row = (lax.axis_index(a).astype(jnp.int32) for a in ("z_hi", "core", "row"))
    upper = row // CUBE
    every = jnp.stack((half, core, row % CUBE, 0 * upper))
    near = jnp.stack((half, core, row % CUBE, 2 * upper))
    far = jnp.stack((half, core, row % CUBE, 2 - 2 * upper))
    quarter = lax.axis_index("quarter")
    quarters = lax.axis_size("quarter")
    rows, depth = left_root.shape
    part = rows // quarters
    grad, right_root = grad[0], right_root[0]

    right_panel = lax.all_gather(right_root, "row", axis=0, tiled=True)
    left_part = lax.dynamic_slice_in_dim(left_root, quarter * part, part, 0)
    cut = (rows + part) // 2
    top = lax.ppermute(grad[:cut], "z_hi", SWAP)
    bottom = lax.ppermute(jnp.concatenate((grad[cut:], left_part)), "z_hi", SWAP)
    mine = with_partner(copies_to_all(jnp.concatenate((grad, left_root)), "y"))
    grad_theirs = copies_to_all(jnp.concatenate((top, bottom[: rows - cut])), "y")
    panel = mine + with_partner(grad_theirs)
    _, left_part = lax.optimization_barrier((grad_theirs, bottom[rows - cut :]))
    left_other = copies_to_all(left_part, "quarter").reshape(rows, depth)

    mixed, *parts = mix(every, panel, (0, 0, 0, 0), right_panel, jnp.bfloat16, 2)
    mixed, parts, left_other = lax.optimization_barrier((mixed, parts, left_other))
    runs = [list(range(i, i + CUBE)) for i in range(0, lax.axis_size("row"), CUBE)]
    near_panel = lax.all_gather(mixed, "row", axis=0, tiled=True, axis_index_groups=runs)
    others = []
    for piece in parts:
        others.append(across(piece))
    left_theirs = copies_to_all(left_other, "y")
    panel = mine + with_partner(left_theirs)
    slots = []
    for piece in others:
        slots.append(far_slots(piece))
    (begun,) = mix(near, panel, (1, 1, 0, 0), near_panel, jnp.float32, 0, (3,))
    renewed, updated = update(far, panel, (1, 1, 0, 0), *slots, begun, momentum[0], weights[0])
    spread = lax.all_to_all(updated.reshape(quarters, part, depth), "quarter", 0, 0, tiled=True)
    return renewed[None], spread


def solution(mesh):
    fine = Mesh(mesh.devices.reshape(4, 8, 4, 2, 2), AXES)
    placed = P("quarter", "row", ("y", "z_hi", "core"))
    return jax.shard_map(
        per_device,
        mesh=fine,
        in_specs=(placed, P("row", ("y", "z_hi", "core")), placed, placed, placed),
        out_specs=(placed, P(None, ("row", "quarter"), ("y", "z_hi", "core"))),
        check_vma=False,
    )
```
